256 devices in a mesh: section: 8 (over y, core), dp: 32 (over z, x).
Axes of the slice: x: 4, y: 4, z: 8, core: 2. Of those that a mesh axis runs over, the one named last changes fastest.
Arguments:
- crop_maps: bfloat16 [32, 4, 2, 8, 8, 640], P('dp'), may hold values from -6 to 6
- target_maps: int32 [32, 4, 2, 8, 8], P('dp'), may hold values 0 or 1
- crop_counts: int32 [32, 4], P('dp'), may hold values from 1 to 2, as said below
- depth_kernels: float32 [8, 49, 640], P('section'), may hold values from -0.875 to 0.875
- weight_in: bfloat16 [8, 640, 2560], P('section', 'dp'), may hold values from -0.25 to 0.25
- weight_out: bfloat16 [8, 2560, 640], P('section', 'dp'), may hold values from -0.125 to 0.125
- head_weight: float32 [640], replicated, may hold values from -0.25 to 0.25
Outputs:
- grad_in: float32 [8, 640, 2560], P('section', 'dp')
- grad_out: float32 [8, 2560, 640], P('section', 'dp')
- grad_kernels: float32 [8, 49, 640], P('section')
- grad_head: float32 [640], replicated
- loss_value: float32 [], replicated
The draws below stay inside these ranges and needn't reach their ends.
Inputs may be any that keep to these rules, and one draw needn't show every extreme that they name: `crop_counts`: every data group has some micro-batch with exactly 2 crops.
All inputs are finite; a program needn't handle non-finite values. No bound on the sum of `target_maps` on one device may be relied on, other than what follows from the above.
Results may differ from the reference program's by a relative error of at most 0.034.
Values may be sent and summed in bfloat16 or wider, within the bound.
No kernel may reach another device: no remote copies, remote signals or barrier semaphores. Data moves between devices by JAX's collectives and lax.ppermute only.
A program may use at most 128 MiB of HBM per device.

```python
import jax
import jax.numpy as jnp
from jax import lax

C = 640
H = 2560
P_SIZE = 8
M = 4
CAP = 2
SECTIONS = 8
GROUPS = 32


def draw_crop_counts(key, part):
    base = jax.random.randint(jax.random.fold_in(key, 11), (GROUPS, M), 1, CAP + 1, dtype=jnp.int32)
    chosen = jax.random.randint(jax.random.fold_in(key, 12), (GROUPS, 1), 0, M, dtype=jnp.int32)
    return jnp.where(jnp.arange(M, dtype=jnp.int32)[None, :] == chosen, CAP, base).astype(jnp.int32)


def touch_ends(array, own_key, smallest, largest):
    longest = array.shape.index(max(array.shape))
    spots = []
    for shift in (0, 1):
        where = [jax.random.randint(jax.random.fold_in(own_key, axis), (), 0, length) for axis, length in enumerate(array.shape)]
        where[longest] = (where[longest] + shift) % array.shape[longest]
        spots.append(tuple(where))
    return array.at[spots[0]].set(smallest).at[spots[1]].set(largest)


def block_scale(rng, shape, split, low, largest):
    def one(position, shards_of):
        draws = jax.random.uniform(jax.random.fold_in(jax.random.fold_in(rng, 6), position), (shards_of,), jnp.float32, low / len(split), largest / len(split))
        return jnp.repeat(jnp.exp(draws), shape[position] // shards_of).reshape((-1,) + (1,) * (len(shape) - position - 1))

    level = one(*split[0])
    for cut in split[1:]:
        level = level * one(*cut)
    return level


def scatter_about(key, dims, scale, most, shards=(), kind=jnp.bfloat16):
    values = jax.random.normal(key, dims, jnp.float32) * scale
    if len(shards) > 0:
        values = block_scale(key, dims, shards, -0.22, 0.18) * values
    return jnp.clip(values, min=-most, max=most).astype(kind)


def setup_inputs(seed: int = 0) -> dict:
    key_of = jax.random.split(jax.random.key(seed), 8)
    crop_maps = scatter_about(key_of[0], (GROUPS, M, CAP, P_SIZE, P_SIZE, C), 1.0, 6.0, ((0, 32),))
    target_maps = touch_ends((jax.random.randint(key_of[1], (GROUPS, M, CAP, P_SIZE, P_SIZE), 0, 5) < 2).astype(jnp.int32), jax.random.fold_in(key_of[1], 1), 0, 1)
    crop_counts = draw_crop_counts(jax.random.fold_in(key_of[7], 71), 0)
    depth_kernels = scatter_about(key_of[3], (SECTIONS, 49, C), 49 ** -0.5, 0.875, ((0, 8),), jnp.float32)
    weight_in = scatter_about(key_of[4], (SECTIONS, C, H), C ** -0.5, 0.25, ((0, 8), (1, 32)))
    weight_out = scatter_about(key_of[5], (SECTIONS, H, C), H ** -0.5, 0.125, ((0, 8), (1, 32)))
    head_weight = scatter_about(key_of[6], (C,), C ** -0.5, 0.25, (), jnp.float32)
    return dict(crop_maps=crop_maps, target_maps=target_maps, crop_counts=crop_counts, depth_kernels=depth_kernels, weight_in=weight_in, weight_out=weight_out, head_weight=head_weight)


EPSILON = 1e-06
SQRT_HALF = 0.7071067811865476
INV_ROOT_TWO_PI = 0.3989422804014327

def depthwise(values, kernel):
    side = values.shape[1]
    padded = jnp.pad(values, ((0, 0), (3, 3), (3, 3), (0, 0)))
    result = jnp.zeros_like(values)
    for vertical in range(7):
        for across in range(7):
            result = result + padded[:, vertical:vertical + side, across:across + side, :] * kernel[vertical * 7 + across]
    return result

def depthwise_back(grads, kernel):
    side = grads.shape[1]
    padded = jnp.pad(grads, ((0, 0), (3, 3), (3, 3), (0, 0)))
    result = jnp.zeros_like(grads)
    for vertical in range(7):
        for across in range(7):
            result = result + padded[:, 6 - vertical:6 - vertical + side, 6 - across:6 - across + side, :] * kernel[vertical * 7 + across]
    return result

def kernel_grad(values, grads):
    side = values.shape[1]
    padded = jnp.pad(values, ((0, 0), (3, 3), (3, 3), (0, 0)))
    taps = []
    for vertical in range(7):
        for across in range(7):
            taps.append(lax.optimization_barrier(jnp.sum(padded[:, vertical:vertical + side, across:across + side, :] * grads, axis=(0, 1, 2))))
    return jnp.stack(taps, axis=0)

def block_parts(tiles, kernel, weight_in):
    width = tiles.shape[-1]
    widened = tiles.astype(jnp.float32)
    mixed = depthwise(widened, kernel).reshape(-1, width)
    centred = mixed - lax.optimization_barrier(jnp.mean(mixed, axis=-1, keepdims=True))
    inverse = lax.rsqrt(lax.optimization_barrier(jnp.mean(centred * centred, axis=-1, keepdims=True)) + EPSILON)
    normed = centred * inverse
    normed_low = normed.astype(jnp.bfloat16)
    hidden = jnp.dot(normed_low, weight_in, preferred_element_type=jnp.float32)
    activated = (hidden * 0.5 * (1.0 + lax.erf(hidden * SQRT_HALF))).astype(jnp.bfloat16)
    return (widened, normed, inverse, normed_low, hidden, activated)

def block_forward(tiles, kernel, weight_in, weight_out):
    width = tiles.shape[-1]
    widened, normed, inverse, normed_low, hidden, activated = block_parts(tiles, kernel, weight_in)
    output = jnp.dot(activated, weight_out, preferred_element_type=jnp.float32)
    return (widened.reshape(-1, width) + output).astype(jnp.bfloat16).reshape(tiles.shape)

def block_backward(tiles, upstream, kernel, weight_in, weight_out):
    width = tiles.shape[-1]
    widened, normed, inverse, normed_low, hidden, activated = block_parts(tiles, kernel, weight_in)
    up_flat = upstream.reshape(-1, width)
    through = lax.dot_general(up_flat, weight_out, (((1,), (1,)), ((), ())), preferred_element_type=jnp.float32)
    slope = 0.5 * (1.0 + lax.erf(hidden * SQRT_HALF)) + hidden * jnp.exp(-0.5 * hidden * hidden) * INV_ROOT_TWO_PI
    hidden_grad = (through * slope).astype(jnp.bfloat16)
    normed_grad = lax.dot_general(hidden_grad, weight_in, (((1,), (1,)), ((), ())), preferred_element_type=jnp.float32)
    mixed_grad = inverse * (normed_grad - lax.optimization_barrier(jnp.mean(normed_grad, axis=-1, keepdims=True)) - normed * lax.optimization_barrier(jnp.mean(normed_grad * normed, axis=-1, keepdims=True)))
    mixed_tiles = mixed_grad.reshape(tiles.shape)
    kernel_term = kernel_grad(widened, mixed_tiles)
    tile_grad = (upstream.astype(jnp.float32) + depthwise_back(mixed_tiles, kernel)).astype(jnp.bfloat16)
    return (tile_grad, kernel_term, normed_low, hidden_grad, activated, up_flat)

def outer_sum(left, right):
    return lax.dot_general(left, right, (((0,), (0,)), ((), ())), preferred_element_type=jnp.float32)

def head_terms(final, targets, live, head_weight, factor):
    widened = final.astype(jnp.float32)
    logits = lax.optimization_barrier(jnp.sum(widened * head_weight, axis=-1))
    weight_live = live.astype(jnp.float32)[:, :, None, None]
    truth = targets.astype(jnp.float32)
    loss_term = jnp.sum(weight_live * (jax.nn.softplus(logits) - truth * logits)) * factor
    logit_grad = (jax.nn.sigmoid(logits) - truth) * weight_live * factor
    seeds = (logit_grad[..., None] * head_weight).astype(jnp.bfloat16)
    head_term = lax.optimization_barrier(jnp.sum(logit_grad[..., None] * widened, axis=(0, 1, 2, 3)))
    return (loss_term, seeds, head_term)

def reference(crop_maps, target_maps, crop_counts, depth_kernels, weight_in, weight_out, head_weight):
    factor = 1.0 / (M * CAP)

    def per_group(carry, group):
        acc_in, acc_out, acc_kernel, acc_head, acc_loss = carry
        crops, targets, counts = group
        live = jnp.arange(CAP)[None, :] < counts[:, None]
        current = (crops * live[:, :, None, None, None].astype(jnp.bfloat16)).reshape(M * CAP, P_SIZE, P_SIZE, C)
        saved = []
        for layer in range(SECTIONS):
            saved.append(current)
            current = block_forward(current, depth_kernels[layer], weight_in[layer], weight_out[layer])
        loss_term, seeds, head_term = head_terms(current.reshape(M, CAP, P_SIZE, P_SIZE, C), targets, live, head_weight, factor)
        upstream = seeds.reshape(M * CAP, P_SIZE, P_SIZE, C)
        for layer in range(SECTIONS - 1, -1, -1):
            upstream, kernel_term, normed_low, hidden_grad, activated, up_flat = block_backward(saved[layer], upstream, depth_kernels[layer], weight_in[layer], weight_out[layer])
            acc_in = acc_in.at[layer].add(outer_sum(normed_low, hidden_grad))
            acc_out = acc_out.at[layer].add(outer_sum(activated, up_flat))
            acc_kernel = acc_kernel.at[layer].add(kernel_term)
        return ((acc_in, acc_out, acc_kernel, acc_head + head_term, acc_loss + loss_term), None)
    start = (jnp.zeros((SECTIONS, C, H), jnp.float32), jnp.zeros((SECTIONS, H, C), jnp.float32), jnp.zeros((SECTIONS, 49, C), jnp.float32), jnp.zeros((C,), jnp.float32), jnp.zeros((), jnp.float32))
    result, _ = lax.scan(per_group, start, (crop_maps, target_maps, crop_counts))
    return (result[0], result[1], result[2], result[3], result[4])
```

```python
import jax
import jax.numpy as jnp
from jax import lax
from jax.experimental import pallas as pl
from jax.experimental.pallas import tpu as pltpu
from jax.sharding import PartitionSpec as P

EPSILON = 1e-06
SQRT_HALF = 0.7071067811865476
INV_ROOT_TWO_PI = 0.3989422804014327
SIDE = 8
REACH = 3
TAPS = 7
LANES = 128
Z_SIZE = 8
X_SIZE = 4
BLOCKS = 2
CHUNK = 512
FORWARD_KEPT = 5
BACKWARD_KEPT = 3
VMEM_LIMIT = 24 * 1024 * 1024
SMALL_LIMIT = 8 * 1024 * 1024


def shifted(rows, offset):
    if offset == 0:
        return rows
    place = lax.broadcasted_iota(jnp.int32, rows.shape, 0) + offset
    moved = pltpu.roll(rows, (-offset) % SIDE, 0)
    return jnp.where((place >= 0) & (place < SIDE), moved, 0.0)


def depthwise_into(source, kernel, target, backward):
    width = source.shape[-1]
    sign = -1 if backward else 1
    for first in range(0, width, LANES):
        lanes = pl.ds(first, LANES)
        rows = [source[pl.ds(y * SIDE, SIDE), lanes] for y in range(SIDE)]
        sums = [None] * SIDE
        for across in range(TAPS):
            moved = [shifted(row, sign * (across - REACH)) for row in rows]
            for vertical in range(TAPS):
                tap = kernel[pl.ds(vertical * TAPS + across, 1), lanes]
                for y in range(SIDE):
                    origin = y + sign * (vertical - REACH)
                    if 0 <= origin < SIDE:
                        term = moved[origin] * tap
                        sums[y] = term if sums[y] is None else sums[y] + term
        for y in range(SIDE):
            target[pl.ds(y * SIDE, SIDE), lanes] = sums[y]


def fetch(control, block, own, other, buffer, semaphore):
    @pl.when(control[1] == block)
    def _():
        pltpu.make_async_copy(own, buffer.at[block], semaphore).start()

    @pl.when(control[1] != block)
    def _():
        pltpu.make_async_copy(other, buffer.at[block], semaphore).start()

    return pltpu.make_async_copy(own, buffer.at[block], semaphore)


def take_tiles(control, own_tiles, arrived, wide):
    @pl.when(control[2] == 1)
    def _():
        wide[...] = own_tiles[...].astype(jnp.float32)

    @pl.when(control[2] != 1)
    def _():
        wide[...] = arrived[...].astype(jnp.float32)


def forward_kernel(
    control, own_tiles, arrived, kernels, own_in, other_in, own_out, other_out, *rest
):
    rest = rest[-(1 + FORWARD_KEPT * 2 + 6):]
    result, rest = rest[0], rest[1:]
    kept_out, rest = rest[:FORWARD_KEPT], rest[FORWARD_KEPT:]
    kept, rest = rest[:FORWARD_KEPT], rest[FORWARD_KEPT:]
    first_buffer, second_buffer, weight_ready, kept_done, wide, mixed = rest
    inputs, lows, inverses, slopes, actives = kept
    expand = own_in.shape[1]
    loads = []
    for block in range(BLOCKS):
        loads.append(
            (
                fetch(control, block, own_in, other_in, first_buffer, weight_ready.at[block, 0]),
                fetch(control, block, own_out, other_out, second_buffer, weight_ready.at[block, 1]),
            )
        )
    stores = []
    take_tiles(control, own_tiles, arrived, wide)
    for block in range(BLOCKS):
        inputs[block] = wide[...].astype(jnp.bfloat16)
        depthwise_into(wide, kernels.at[block], mixed, False)
        values = mixed[...]
        centred = values - jnp.mean(values, axis=-1, keepdims=True)
        inverse = lax.rsqrt(jnp.mean(centred * centred, axis=-1, keepdims=True) + EPSILON)
        inverses[block] = jnp.broadcast_to(inverse, inverses.shape[1:])
        low = (centred * inverse).astype(jnp.bfloat16)
        lows[block] = low
        loads[block][0].wait()
        total = jnp.zeros(wide.shape, jnp.float32)
        for start in range(0, expand, CHUNK):
            part = slice(start, start + CHUNK)
            hidden = jnp.dot(low, first_buffer[block, :, part], preferred_element_type=jnp.float32)
            half = 0.5 * (1.0 + lax.erf(hidden * SQRT_HALF))
            active = (hidden * half).astype(jnp.bfloat16)
            slope = half + hidden * jnp.exp(-0.5 * hidden * hidden) * INV_ROOT_TWO_PI
            slopes[block, :, part] = slope.astype(jnp.bfloat16)
            actives[block, :, part] = active
            if start == 0:
                loads[block][1].wait()
            total = total + jnp.dot(
                active, second_buffer[block, part, :], preferred_element_type=jnp.float32
            )
        wide[...] = (wide[...] + total).astype(jnp.bfloat16).astype(jnp.float32)
        for index in range(FORWARD_KEPT):
            copy = pltpu.make_async_copy(
                kept[index].at[block], kept_out[index].at[block, control[0]], kept_done.at[block, index]
            )
            copy.start()
            stores.append(copy)
    result[...] = wide[...].astype(jnp.bfloat16)
    for copy in stores:
        copy.wait()


def backward_kernel(
    control, seeds, arrived, kernels, lows_all, inverses_all, slopes_all,
    own_in, other_in, own_out, other_out, *rest
):
    rest = rest[-(1 + BACKWARD_KEPT * 2 + 10):]
    result, rest = rest[0], rest[1:]
    kept_out, rest = rest[:BACKWARD_KEPT], rest[BACKWARD_KEPT:]
    kept, rest = rest[:BACKWARD_KEPT], rest[BACKWARD_KEPT:]
    lows, inverses, slopes, known_ready = rest[:4]
    first_buffer, second_buffer, weight_ready, kept_done, wide, spread = rest[4:]
    ups, hiddens, mixeds = kept
    expand = own_in.shape[1]
    loads = [None] * BLOCKS
    for block in range(BLOCKS - 1, -1, -1):
        second = fetch(control, block, own_out, other_out, second_buffer, weight_ready.at[block, 1])
        known = []
        for index, (source, target) in enumerate(
            ((slopes_all, slopes), (lows_all, lows), (inverses_all, inverses))
        ):
            copy = pltpu.make_async_copy(
                source.at[block, control[0]], target.at[block], known_ready.at[block, index]
            )
            copy.start()
            known.append(copy)
        first = fetch(control, block, own_in, other_in, first_buffer, weight_ready.at[block, 0])
        loads[block] = (second, known, first)
    stores = []
    across = (((1,), (1,)), ((), ()))
    take_tiles(control, seeds, arrived, wide)
    for block in range(BLOCKS - 1, -1, -1):
        second, known, first = loads[block]
        low = wide[...].astype(jnp.bfloat16)
        ups[block] = low
        total = jnp.zeros(wide.shape, jnp.float32)
        second.wait()
        for copy in known:
            copy.wait()
        for start in range(0, expand, CHUNK):
            part = slice(start, start + CHUNK)
            through = lax.dot_general(
                low, second_buffer[block, part, :], across, preferred_element_type=jnp.float32
            )
            grads = (through * slopes[block, :, part].astype(jnp.float32)).astype(jnp.bfloat16)
            hiddens[block, :, part] = grads
            if start == 0:
                first.wait()
            total = total + lax.dot_general(
                grads, first_buffer[block, :, part], across, preferred_element_type=jnp.float32
            )
        normed = lows[block].astype(jnp.float32)
        mixeds[block] = inverses[block][:, :1] * (
            total
            - jnp.mean(total, axis=-1, keepdims=True)
            - normed * jnp.mean(total * normed, axis=-1, keepdims=True)
        )
        depthwise_into(mixeds.at[block], kernels.at[block], spread, True)
        wide[...] = (wide[...] + spread[...]).astype(jnp.bfloat16).astype(jnp.float32)
        for index in range(BACKWARD_KEPT):
            copy = pltpu.make_async_copy(
                kept[index].at[block], kept_out[index].at[block, control[0]], kept_done.at[block, index]
            )
            copy.start()
            stores.append(copy)
    result[...] = wide[...].astype(jnp.bfloat16)
    for copy in stores:
        copy.wait()


def taps_kernel(inputs, mixed, result):
    crops = inputs.shape[1]
    for across in range(TAPS):
        sums = [None] * TAPS
        for crop in range(crops):
            rows = [
                inputs[0, crop, pl.ds(y * SIDE, SIDE), :].astype(jnp.float32) for y in range(SIDE)
            ]
            moved = [
                shifted(mixed[0, crop, pl.ds(y * SIDE, SIDE), :], REACH - across)
                for y in range(SIDE)
            ]
            for vertical in range(TAPS):
                for y in range(SIDE):
                    origin = y - (vertical - REACH)
                    if 0 <= origin < SIDE:
                        term = rows[y] * moved[origin]
                        known = sums[vertical]
                        sums[vertical] = term if known is None else known + term
        for vertical in range(TAPS):
            result[0, pl.ds(vertical * TAPS + across, 1), :] = jnp.sum(
                sums[vertical], axis=0, keepdims=True
            )


def call_stage(kernel, name, control, fixed, known, weights, saved, saved_shapes, out_shape):
    scalar = pl.BlockSpec(memory_space=pltpu.SMEM)
    near = pl.BlockSpec(memory_space=pltpu.VMEM)
    far = pl.BlockSpec(memory_space=pl.ANY)
    operands = [control, *fixed, *known, *weights]
    in_specs = [scalar] + [near] * len(fixed) + [far] * (len(known) + len(weights))
    aliases = {}
    if saved is not None:
        for index, value in enumerate(saved):
            aliases[len(operands)] = 1 + index
            operands.append(value)
            in_specs.append(far)

    def buffer(value):
        return pltpu.VMEM((BLOCKS,) + value.shape[2:], value.dtype)

    scratch = [buffer(value) for value in saved_shapes]
    if known:
        lows, inverses, slopes = known
        scratch += [buffer(lows), buffer(inverses), buffer(slopes)]
        scratch += [pltpu.SemaphoreType.DMA((BLOCKS, len(known)))]
    scratch += [
        pltpu.VMEM((BLOCKS,) + weights[0].shape, weights[0].dtype),
        pltpu.VMEM((BLOCKS,) + weights[2].shape, weights[2].dtype),
        pltpu.SemaphoreType.DMA((BLOCKS, 2)),
        pltpu.SemaphoreType.DMA((BLOCKS, len(saved_shapes))),
        pltpu.VMEM(out_shape.shape, jnp.float32),
        pltpu.VMEM(out_shape.shape, jnp.float32),
    ]
    outputs = pl.pallas_call(
        kernel,
        name=name,
        out_shape=[out_shape, *saved_shapes],
        in_specs=in_specs,
        out_specs=[near] + [far] * len(saved_shapes),
        scratch_shapes=scratch,
        input_output_aliases=aliases,
        compiler_params=pltpu.CompilerParams(vmem_limit_bytes=VMEM_LIMIT),
    )(*operands)
    return outputs[0], tuple(outputs[1:])


def tap_grads(inputs, mixed):
    blocks, crops, cells, width = inputs.shape
    window = pl.BlockSpec((1, crops - 1, cells, LANES), lambda block, lane: (block, 0, 0, lane))
    return pl.pallas_call(
        taps_kernel,
        name="taps",
        out_shape=jax.ShapeDtypeStruct((blocks, TAPS * TAPS, width), jnp.float32),
        grid=(blocks, width // LANES),
        in_specs=[window, window],
        out_specs=pl.BlockSpec((1, TAPS * TAPS, LANES), lambda block, lane: (block, 0, lane)),
        compiler_params=pltpu.CompilerParams(vmem_limit_bytes=SMALL_LIMIT),
    )(inputs, mixed)


def head_kernel(*refs):
    finals, (truth, live, weight, seeds, rows) = refs[:-5], refs[-5:]
    factor = 1.0 / (BLOCKS * len(finals))
    head_term = jnp.zeros(weight.shape, jnp.float32)
    loss_term = jnp.zeros((1, 1), jnp.float32)
    for crop, final in enumerate(finals):
        cells = pl.ds(crop * SIDE * SIDE, SIDE * SIDE)
        widened = final[...].astype(jnp.float32)
        logits = jnp.sum(widened * weight[...], axis=-1, keepdims=True)
        softplus = jnp.maximum(logits, 0.0) + jnp.log1p(jnp.exp(-jnp.abs(logits)))
        loss = live[cells, :] * (softplus - truth[cells, :] * logits)
        loss_term = loss_term + jnp.sum(loss, axis=0, keepdims=True) * factor
        grads = (jax.nn.sigmoid(logits) - truth[cells, :]) * live[cells, :] * factor
        seeds[crop] = (grads * weight[...]).astype(jnp.bfloat16)
        head_term = head_term + jnp.sum(grads * widened, axis=0, keepdims=True)
    place = lax.broadcasted_iota(jnp.int32, rows.shape, 0)
    rows[...] = jnp.where(place == 0, head_term, jnp.where(place == 1, loss_term, 0.0))


def assemble_kernel(control, *refs):
    pieces, result, ready = refs[:-2], refs[-2], refs[-1]
    copies = []
    for first, piece in enumerate(pieces):
        for second in range(piece.shape[0]):
            if len(pieces) == Z_SIZE:
                target = (control[0] - first) % Z_SIZE * X_SIZE + (control[1] - second) % X_SIZE
            else:
                target = (control[0] - second) % Z_SIZE * X_SIZE + (control[1] - first) % X_SIZE
            copy = pltpu.make_async_copy(
                piece.at[second], result.at[target], ready.at[first, second]
            )
            copy.start()
            copies.append(copy)
    for copy in copies:
        copy.wait()


def assemble(control, pieces):
    piece = pieces[0]
    far = pl.BlockSpec(memory_space=pl.ANY)
    return pl.pallas_call(
        assemble_kernel,
        name="assemble",
        out_shape=jax.ShapeDtypeStruct((Z_SIZE * X_SIZE,) + piece.shape[1:], piece.dtype),
        in_specs=[pl.BlockSpec(memory_space=pltpu.SMEM)] + [far] * len(pieces),
        out_specs=far,
        scratch_shapes=[pltpu.SemaphoreType.DMA((len(pieces), piece.shape[0]))],
        compiler_params=pltpu.CompilerParams(vmem_limit_bytes=SMALL_LIMIT),
    )(control, *pieces)


def along_x(value, steps):
    pairs = [
        (z * X_SIZE + x, z * X_SIZE + (x + steps) % X_SIZE)
        for z in range(Z_SIZE)
        for x in range(X_SIZE)
    ]
    return lax.ppermute(value, "dp", pairs)


def along_z(value, steps):
    pairs = [
        (z * X_SIZE + x, (z + steps) % Z_SIZE * X_SIZE + x)
        for z in range(Z_SIZE)
        for x in range(X_SIZE)
    ]
    return lax.ppermute(value, "dp", pairs)


def gather_x(value):
    return [value] + [along_x(value, steps) for steps in range(1, X_SIZE)]


def gather_z(value):
    half = Z_SIZE // 2
    behind = [value]
    for _ in range(half):
        behind.append(along_z(behind[-1], 1))
    ahead = [value]
    for _ in range(half - 1):
        ahead.append(along_z(ahead[-1], -1))
    return behind + ahead[:0:-1]


def picker(blocks, axis, home):
    count = blocks.shape[axis]
    return lambda steps: lax.dynamic_index_in_dim(
        blocks, (home + steps) % count, axis, keepdims=False
    )


def reduce_x(blocks, axis, home):
    block = picker(blocks, axis, home)
    arrivals = [along_x(block(steps), steps) for steps in range(1, X_SIZE)]
    total = block(0).astype(jnp.float32)
    for arrival in arrivals:
        total = total + arrival.astype(jnp.float32)
    return total


def reduce_z(blocks, axis, home):
    block = picker(blocks, axis, home)
    half = Z_SIZE // 2
    add = lambda left, right: left.astype(jnp.float32) + right.astype(jnp.float32)
    behind, ahead = block(half), block(1 - half)
    for steps in range(half - 1, 0, -1):
        behind = add(along_z(behind, 1), block(steps)).astype(jnp.bfloat16)
    for steps in range(half - 2, 0, -1):
        ahead = add(along_z(ahead, -1), block(-steps)).astype(jnp.bfloat16)
    return add(along_z(behind, 1), block(0)) + along_z(ahead, -1).astype(jnp.float32)


def all_sum(value, axis):
    count = lax.axis_size(axis)
    step = 1
    while step < count:
        value = value + lax.ppermute(value, axis, [(place, place ^ step) for place in range(count)])
        step *= 2
    return value


def outer_sum(left, right):
    return lax.dot_general(
        left, right, (((0, 1), (0, 1)), ((), ())), preferred_element_type=jnp.float32
    )


def body(crop_maps, target_maps, crop_counts, depth_kernels, weight_in, weight_out, head_weight):
    section = lax.axis_index("section")
    sections = lax.axis_size("section")
    stages = sections // BLOCKS
    stage = section // BLOCKS
    core = section % BLOCKS
    micros, slots = crop_maps.shape[1:3]
    width = crop_maps.shape[-1]
    cells = SIDE * SIDE
    other = [(index, index ^ 1) for index in range(sections)]
    onward = [(index, index + BLOCKS) for index in range(sections - BLOCKS)]
    back = [(index + BLOCKS, index) for index in range(sections - BLOCKS)]

    group = lax.axis_index("dp")
    home_z, home_x = group // X_SIZE, group % X_SIZE
    home = jnp.stack([home_z, home_x]).astype(jnp.int32)
    shard_rows, expand = weight_in.shape[1:]
    first_shard = weight_in[0].reshape(shard_rows * expand // LANES, LANES)
    first_pieces = gather_z(jnp.stack(gather_x(first_shard)))
    second_pieces = gather_x(jnp.stack(gather_z(weight_out[0])))
    own_in = assemble(home, first_pieces).reshape(width, expand)
    own_out = assemble(home, second_pieces).reshape(expand, width)
    other_in = lax.ppermute(own_in, "section", other)
    other_out = lax.ppermute(own_out, "section", other)
    weights = (own_in, other_in, own_out, other_out)
    other_kernel = lax.ppermute(depth_kernels[0], "section", other)
    first_kernel = jnp.where(core == 0, depth_kernels[0], other_kernel)
    second_kernel = jnp.where(core == 0, other_kernel, depth_kernels[0])
    kernels = jnp.stack([first_kernel, second_kernel])

    crops = micros * slots // BLOCKS
    live = (jnp.arange(slots)[None, :] < crop_counts[0][:, None]).reshape(crops, BLOCKS)
    pick = lambda value: lax.dynamic_index_in_dim(value, core, 1, keepdims=False)
    own_live = pick(live).astype(jnp.float32)[:, None]
    own_crops = pick(crop_maps[0].reshape(crops, BLOCKS, cells, width))
    own_targets = pick(target_maps[0].reshape(crops, BLOCKS, cells))
    entering = own_crops * own_live[:, :, None].astype(jnp.bfloat16)

    ticks = crops + stages - 1
    spare = crops

    def kept(*tail, dtype):
        return jax.ShapeDtypeStruct((BLOCKS, crops + 1, cells) + tail, dtype)

    tile_shape = jax.ShapeDtypeStruct((cells, width), jnp.bfloat16)
    forward_shapes = [
        kept(width, dtype=jnp.bfloat16),
        kept(width, dtype=jnp.bfloat16),
        kept(LANES, dtype=jnp.float32),
        kept(expand, dtype=jnp.bfloat16),
        kept(expand, dtype=jnp.bfloat16),
    ]
    saved = None
    arrived = entering[0]
    finals = []
    for moment in range(ticks):
        micro = moment - stage
        place = jnp.where((micro >= 0) & (micro < crops), micro, spare)
        control = jnp.stack([place, core, stage == 0]).astype(jnp.int32)
        result, saved = call_stage(
            forward_kernel, "forward", control,
            [entering[min(moment, crops - 1)], arrived, kernels], [], weights,
            saved, forward_shapes, tile_shape,
        )
        if moment >= stages - 1:
            finals.append(result)
        if moment < ticks - 1:
            arrived = lax.ppermute(result, "section", onward)
    inputs, lows, inverse, slope, active = saved

    is_last = stage == stages - 1
    by_cell = lambda value: value.reshape(crops * cells, 1).astype(jnp.float32)
    seeds, head_rows = pl.pallas_call(
        head_kernel,
        name="head",
        out_shape=[
            jax.ShapeDtypeStruct((crops, cells, width), jnp.bfloat16),
            jax.ShapeDtypeStruct((SIDE, width), jnp.float32),
        ],
        compiler_params=pltpu.CompilerParams(vmem_limit_bytes=SMALL_LIMIT),
    )(
        *finals,
        by_cell(own_targets),
        by_cell(jnp.broadcast_to(own_live, own_targets.shape)),
        head_weight[None],
    )
    head_rows = all_sum(jnp.where(is_last, head_rows, 0.0), "section")

    backward_shapes = [
        kept(width, dtype=jnp.bfloat16),
        kept(expand, dtype=jnp.bfloat16),
        kept(width, dtype=jnp.float32),
    ]
    grads = None
    arrived = seeds[0]
    for moment in range(ticks):
        micro = moment - (stages - 1 - stage)
        place = jnp.where((micro >= 0) & (micro < crops), micro, spare)
        control = jnp.stack([place, core, is_last]).astype(jnp.int32)
        result, grads = call_stage(
            backward_kernel, "backward", control,
            [seeds[min(moment, crops - 1)], arrived, kernels],
            [lows, inverse, slope], weights, grads, backward_shapes, tile_shape,
        )
        if moment < ticks - 1:
            arrived = lax.ppermute(result, "section", back)
    ups, hidden_grads, mixed_grads = grads

    def block_of(value, which):
        return lax.dynamic_index_in_dim(value, which, 0, keepdims=False)[:crops]

    def outer_pair(which):
        return (
            outer_sum(block_of(lows, which), block_of(hidden_grads, which)),
            outer_sum(block_of(active, which), block_of(ups, which)),
        )

    away_in, away_out = (value.astype(jnp.bfloat16) for value in outer_pair(1 - core))
    came_in = lax.ppermute(away_in, "section", other)
    came_out = lax.ppermute(away_out, "section", other)
    home_in, home_out = outer_pair(core)
    by_group = lambda value, *tail: value.astype(jnp.bfloat16).reshape((Z_SIZE, X_SIZE) + tail)
    sum_out = by_group(home_out + came_out.astype(jnp.float32), expand // Z_SIZE // X_SIZE, width)
    sum_in = by_group(home_in + came_in.astype(jnp.float32), *first_shard.shape)
    second_part = reduce_z(sum_out, 0, home_z).astype(jnp.bfloat16)
    first_part = reduce_x(sum_in, 1, home_x).astype(jnp.bfloat16)
    second_part = reduce_x(second_part, 0, home_x)
    first_part = reduce_z(first_part, 0, home_z).reshape(shard_rows, expand)

    taps = tap_grads(inputs, mixed_grads)
    tap_away = lax.dynamic_index_in_dim(taps, 1 - core, 0, keepdims=False)
    tap_home = lax.dynamic_index_in_dim(taps, core, 0, keepdims=False)
    tap_sum = tap_home + lax.ppermute(tap_away, "section", other)
    small = all_sum(jnp.concatenate([tap_sum, head_rows[:2]]), "dp")
    tap_count = TAPS * TAPS
    return (
        first_part[None],
        second_part[None],
        small[None, :tap_count],
        small[tap_count],
        small[tap_count + 1, 0],
    )


def solution(mesh):
    return jax.shard_map(
        body,
        mesh=mesh,
        in_specs=(
            P("dp", None, None, None, None, None),
            P("dp", None, None, None, None),
            P("dp", None),
            P("section", None, None),
            P("section", "dp", None),
            P("section", "dp", None),
            P(),
        ),
        out_specs=(
            P("section", "dp", None),
            P("section", "dp", None),
            P("section", None, None),
            P(),
            P(),
        ),
        check_vma=False,
    )
```

```python
import jax
import jax.numpy as jnp
from jax import lax
from jax.experimental import pallas as pl
from jax.experimental.pallas import tpu as pltpu
from jax.sharding import PartitionSpec as P

EPSILON = 1e-06
SQRT_HALF = 0.7071067811865476
INV_ROOT_TWO_PI = 0.3989422804014327
SIDE = 8
REACH = 3
TAPS = 7
LANES = 128
Z_SIZE = 8
X_SIZE = 4
BLOCKS = 2
STEP_CROPS = 2
CHUNK = 1280
RIDERS = 16
FORWARD_KEPT = 5
BACKWARD_KEPT = 3
VMEM_LIMIT = 48 * 1024 * 1024
SMALL_LIMIT = 8 * 1024 * 1024


def shifted(rows, offset):
    if offset == 0:
        return rows
    place = lax.broadcasted_iota(jnp.int32, rows.shape, 0) + offset
    moved = pltpu.roll(rows, (-offset) % SIDE, 0)
    return jnp.where((place >= 0) & (place < SIDE), moved, 0.0)


def depthwise_into(source, kernel, target, backward):
    cells, width = source.shape
    sign = -1 if backward else 1
    for start in range(0, cells, SIDE * SIDE):
        for first in range(0, width, LANES):
            lanes = pl.ds(first, LANES)
            rows = [source[pl.ds(start + y * SIDE, SIDE), lanes] for y in range(SIDE)]
            sums = [None] * SIDE
            for across in range(TAPS):
                moved = [shifted(row, sign * (across - REACH)) for row in rows]
                for vertical in range(TAPS):
                    tap = kernel[pl.ds(vertical * TAPS + across, 1), lanes]
                    for y in range(SIDE):
                        origin = y + sign * (vertical - REACH)
                        if 0 <= origin < SIDE:
                            term = moved[origin] * tap
                            sums[y] = term if sums[y] is None else sums[y] + term
            for y in range(SIDE):
                target[pl.ds(start + y * SIDE, SIDE), lanes] = sums[y]


def fetch(control, block, own, other, buffer, semaphore):
    @pl.when(control[1] == block)
    def _():
        pltpu.make_async_copy(own, buffer.at[block], semaphore).start()

    @pl.when(control[1] != block)
    def _():
        pltpu.make_async_copy(other, buffer.at[block], semaphore).start()

    return pltpu.make_async_copy(own, buffer.at[block], semaphore)


def take_tiles(control, own_tiles, arrived, wide):
    @pl.when(control[2] == 1)
    def _():
        wide[...] = own_tiles[: wide.shape[0], :].astype(jnp.float32)

    @pl.when(control[2] != 1)
    def _():
        wide[...] = arrived[: wide.shape[0], :].astype(jnp.float32)


def forward_kernel(
    control, own_tiles, arrived, kernels, own_in, other_in, own_out, other_out, *rest
):
    rest = rest[-(1 + FORWARD_KEPT * 2 + 6):]
    result, rest = rest[0], rest[1:]
    kept_out, rest = rest[:FORWARD_KEPT], rest[FORWARD_KEPT:]
    kept, rest = rest[:FORWARD_KEPT], rest[FORWARD_KEPT:]
    first_buffer, second_buffer, weight_ready, kept_done, wide, mixed = rest
    inputs, lows, inverses, slopes, actives = kept
    expand = own_in.shape[1]
    loads = []
    for block in range(BLOCKS):
        loads.append(
            (
                fetch(control, block, own_in, other_in, first_buffer, weight_ready.at[block, 0]),
                fetch(control, block, own_out, other_out, second_buffer, weight_ready.at[block, 1]),
            )
        )
    stores = []
    take_tiles(control, own_tiles, arrived, wide)
    for block in range(BLOCKS):
        inputs[block] = wide[...].astype(jnp.bfloat16)
        depthwise_into(wide, kernels.at[block], mixed, False)
        values = mixed[...]
        centred = values - jnp.mean(values, axis=-1, keepdims=True)
        inverse = lax.rsqrt(jnp.mean(centred * centred, axis=-1, keepdims=True) + EPSILON)
        inverses[block] = jnp.broadcast_to(inverse, inverses.shape[1:])
        low = (centred * inverse).astype(jnp.bfloat16)
        lows[block] = low
        loads[block][0].wait()
        total = jnp.zeros(wide.shape, jnp.float32)
        for start in range(0, expand, CHUNK):
            part = slice(start, start + CHUNK)
            hidden = jnp.dot(low, first_buffer[block, :, part], preferred_element_type=jnp.float32)
            half = 0.5 * (1.0 + lax.erf(hidden * SQRT_HALF))
            active = (hidden * half).astype(jnp.bfloat16)
            slope = half + hidden * jnp.exp(-0.5 * hidden * hidden) * INV_ROOT_TWO_PI
            slopes[block, :, part] = slope.astype(jnp.bfloat16)
            actives[block, :, part] = active
            if start == 0:
                loads[block][1].wait()
            total = total + jnp.dot(
                active, second_buffer[block, part, :], preferred_element_type=jnp.float32
            )
        wide[...] = (wide[...] + total).astype(jnp.bfloat16).astype(jnp.float32)
        for index in range(FORWARD_KEPT):
            copy = pltpu.make_async_copy(
                kept[index].at[block], kept_out[index].at[block, control[0]], kept_done.at[block, index]
            )
            copy.start()
            stores.append(copy)
    result[...] = wide[...].astype(jnp.bfloat16)
    for copy in stores:
        copy.wait()


def backward_kernel(
    control, seeds, arrived, kernels, lows_all, inverses_all, slopes_all,
    own_in, other_in, own_out, other_out, *rest
):
    rest = rest[-(1 + BACKWARD_KEPT * 2 + 10):]
    result, rest = rest[0], rest[1:]
    kept_out, rest = rest[:BACKWARD_KEPT], rest[BACKWARD_KEPT:]
    kept, rest = rest[:BACKWARD_KEPT], rest[BACKWARD_KEPT:]
    lows, inverses, slopes, known_ready = rest[:4]
    first_buffer, second_buffer, weight_ready, kept_done, wide, spread = rest[4:]
    ups, hiddens, mixeds = kept
    expand = own_in.shape[1]
    loads = [None] * BLOCKS
    for block in range(BLOCKS - 1, -1, -1):
        second = fetch(control, block, own_out, other_out, second_buffer, weight_ready.at[block, 1])
        known = []
        for index, (source, target) in enumerate(
            ((slopes_all, slopes), (lows_all, lows), (inverses_all, inverses))
        ):
            copy = pltpu.make_async_copy(
                source.at[block, control[0]], target.at[block], known_ready.at[block, index]
            )
            copy.start()
            known.append(copy)
        first = fetch(control, block, own_in, other_in, first_buffer, weight_ready.at[block, 0])
        loads[block] = (second, known, first)
    stores = []
    across = (((1,), (1,)), ((), ()))
    take_tiles(control, seeds, arrived, wide)
    for block in range(BLOCKS - 1, -1, -1):
        second, known, first = loads[block]
        low = wide[...].astype(jnp.bfloat16)
        ups[block] = low
        total = jnp.zeros(wide.shape, jnp.float32)
        second.wait()
        for copy in known:
            copy.wait()
        for start in range(0, expand, CHUNK):
            part = slice(start, start + CHUNK)
            through = lax.dot_general(
                low, second_buffer[block, part, :], across, preferred_element_type=jnp.float32
            )
            grads = (through * slopes[block, :, part].astype(jnp.float32)).astype(jnp.bfloat16)
            hiddens[block, :, part] = grads
            if start == 0:
                first.wait()
            total = total + lax.dot_general(
                grads, first_buffer[block, :, part], across, preferred_element_type=jnp.float32
            )
        normed = lows[block].astype(jnp.float32)
        mixeds[block] = inverses[block][:, :1] * (
            total
            - jnp.mean(total, axis=-1, keepdims=True)
            - normed * jnp.mean(total * normed, axis=-1, keepdims=True)
        )
        depthwise_into(mixeds.at[block], kernels.at[block], spread, True)
        wide[...] = (wide[...] + spread[...]).astype(jnp.bfloat16).astype(jnp.float32)
        for index in range(BACKWARD_KEPT):
            copy = pltpu.make_async_copy(
                kept[index].at[block], kept_out[index].at[block, control[0]], kept_done.at[block, index]
            )
            copy.start()
            stores.append(copy)
    cells = wide.shape[0]
    result[:cells, :] = wide[...].astype(jnp.bfloat16)

    @pl.when(control[2] == 1)
    def _():
        result[cells:, :] = seeds[cells:, :]

    @pl.when(control[2] != 1)
    def _():
        result[cells:, :] = arrived[cells:, :]

    for copy in stores:
        copy.wait()


def taps_kernel(inputs, mixed, result):
    steps, cells = inputs.shape[1:3]
    tile = SIDE * SIDE
    for across in range(TAPS):
        sums = [None] * TAPS
        for step in range(steps):
            for start in range(0, cells, tile):
                strips = [pl.ds(start + y * SIDE, SIDE) for y in range(SIDE)]
                rows = [inputs[0, step, strip, :].astype(jnp.float32) for strip in strips]
                moved = [shifted(mixed[0, step, strip, :], REACH - across) for strip in strips]
                for vertical in range(TAPS):
                    for y in range(SIDE):
                        origin = y - (vertical - REACH)
                        if 0 <= origin < SIDE:
                            term = rows[y] * moved[origin]
                            known = sums[vertical]
                            sums[vertical] = term if known is None else known + term
        for vertical in range(TAPS):
            result[0, pl.ds(vertical * TAPS + across, 1), :] = jnp.sum(
                sums[vertical], axis=0, keepdims=True
            )


def call_stage(kernel, name, control, fixed, known, weights, saved, saved_shapes, out_shape):
    scalar = pl.BlockSpec(memory_space=pltpu.SMEM)
    near = pl.BlockSpec(memory_space=pltpu.VMEM)
    far = pl.BlockSpec(memory_space=pl.ANY)
    operands = [control, *fixed, *known, *weights]
    in_specs = [scalar] + [near] * len(fixed) + [far] * (len(known) + len(weights))
    aliases = {}
    if saved is not None:
        for index, value in enumerate(saved):
            aliases[len(operands)] = 1 + index
            operands.append(value)
            in_specs.append(far)

    def buffer(value):
        return pltpu.VMEM((BLOCKS,) + value.shape[2:], value.dtype)

    scratch = [buffer(value) for value in saved_shapes]
    if known:
        lows, inverses, slopes = known
        scratch += [buffer(lows), buffer(inverses), buffer(slopes)]
        scratch += [pltpu.SemaphoreType.DMA((BLOCKS, len(known)))]
    scratch += [
        pltpu.VMEM((BLOCKS,) + weights[0].shape, weights[0].dtype),
        pltpu.VMEM((BLOCKS,) + weights[2].shape, weights[2].dtype),
        pltpu.SemaphoreType.DMA((BLOCKS, 2)),
        pltpu.SemaphoreType.DMA((BLOCKS, len(saved_shapes))),
        pltpu.VMEM((saved_shapes[0].shape[2], out_shape.shape[1]), jnp.float32),
        pltpu.VMEM((saved_shapes[0].shape[2], out_shape.shape[1]), jnp.float32),
    ]
    outputs = pl.pallas_call(
        kernel,
        name=name,
        out_shape=[out_shape, *[pltpu.HBM(value.shape, value.dtype) for value in saved_shapes]],
        in_specs=in_specs,
        out_specs=[near] + [far] * len(saved_shapes),
        scratch_shapes=scratch,
        input_output_aliases=aliases,
        compiler_params=pltpu.CompilerParams(vmem_limit_bytes=VMEM_LIMIT),
    )(*operands)
    return outputs[0], tuple(outputs[1:])


def tap_grads(inputs, mixed):
    blocks, crops, cells, width = inputs.shape
    window = pl.BlockSpec((1, crops - 1, cells, LANES), lambda block, lane: (block, 0, 0, lane))
    return pl.pallas_call(
        taps_kernel,
        name="taps",
        out_shape=jax.ShapeDtypeStruct((blocks, TAPS * TAPS, width), jnp.float32),
        grid=(blocks, width // LANES),
        in_specs=[window, window],
        out_specs=pl.BlockSpec((1, TAPS * TAPS, LANES), lambda block, lane: (block, 0, lane)),
        compiler_params=pltpu.CompilerParams(vmem_limit_bytes=SMALL_LIMIT),
    )(inputs, mixed)


def head_kernel(*refs):
    finals, (truth, live, weight, seeds) = refs[:-4], refs[-4:]
    step_cells = finals[0].shape[0]
    factor = SIDE * SIDE / (BLOCKS * len(finals) * step_cells)
    head_term = jnp.zeros(weight.shape, jnp.float32)
    loss_term = jnp.zeros((1, 1), jnp.float32)
    for crop, final in enumerate(finals):
        cells = pl.ds(crop * step_cells, step_cells)
        widened = final[...].astype(jnp.float32)
        logits = jnp.sum(widened * weight[...], axis=-1, keepdims=True)
        softplus = jnp.maximum(logits, 0.0) + jnp.log1p(jnp.exp(-jnp.abs(logits)))
        loss = live[cells, :] * (softplus - truth[cells, :] * logits)
        loss_term = loss_term + jnp.sum(loss, axis=0, keepdims=True) * factor
        grads = (jax.nn.sigmoid(logits) - truth[cells, :]) * live[cells, :] * factor
        seeds[crop, :step_cells, :] = (grads * weight[...]).astype(jnp.bfloat16)
        head_term = head_term + jnp.sum(grads * widened, axis=0, keepdims=True)
    place = lax.broadcasted_iota(jnp.int32, (RIDERS, weight.shape[1]), 0)
    riders = jnp.where(place < 2, head_term, jnp.where(place < 4, loss_term, 0.0))
    coarse = riders.astype(jnp.bfloat16)
    rest = (riders - coarse.astype(jnp.float32)).astype(jnp.bfloat16)
    riders = jnp.where(place % 2 == 0, coarse, rest)
    for crop in range(len(finals)):
        seeds[crop, step_cells:, :] = riders


def assemble(control, pieces, distances):
    def kernel(control, *refs):
        sources, result, ready = refs[:-2], refs[-2], refs[-1]
        copies = []
        for source, shards in zip(sources, distances):
            for index, (z_steps, x_steps) in enumerate(shards):
                target = (control[0] - z_steps) % Z_SIZE * X_SIZE + (control[1] - x_steps) % X_SIZE
                copy = pltpu.make_async_copy(
                    source.at[index], result.at[target], ready.at[len(copies)]
                )
                copy.start()
                copies.append(copy)
        for copy in copies:
            copy.wait()

    piece = pieces[0]
    far = pl.BlockSpec(memory_space=pl.ANY)
    return pl.pallas_call(
        kernel,
        name="assemble",
        out_shape=jax.ShapeDtypeStruct((Z_SIZE * X_SIZE,) + piece.shape[1:], piece.dtype),
        in_specs=[pl.BlockSpec(memory_space=pltpu.SMEM)] + [far] * len(pieces),
        out_specs=far,
        scratch_shapes=[pltpu.SemaphoreType.DMA((Z_SIZE * X_SIZE,))],
        compiler_params=pltpu.CompilerParams(vmem_limit_bytes=SMALL_LIMIT),
    )(control, *pieces)


def along_x(value, steps):
    pairs = [
        (z * X_SIZE + x, z * X_SIZE + (x + steps) % X_SIZE)
        for z in range(Z_SIZE)
        for x in range(X_SIZE)
    ]
    return lax.ppermute(value, "dp", pairs)


def along_z(value, steps):
    pairs = [
        (z * X_SIZE + x, (z + steps) % Z_SIZE * X_SIZE + x)
        for z in range(Z_SIZE)
        for x in range(X_SIZE)
    ]
    return lax.ppermute(value, "dp", pairs)


def spread_x(value):
    return [value] + [along_x(value, steps) for steps in range(1, X_SIZE)]


def spread_z(value):
    return [value] + [along_z(value, steps) for steps in range(1, Z_SIZE)]


def chain_x(value):
    half = value.shape[0] // 2
    behind, ahead = along_x(value, 1), along_x(value, -1)
    return [value, behind, along_x(behind[:half], 1), along_x(ahead[half:], -1), ahead]


def chain_z(value):
    half = Z_SIZE // 2
    behind, ahead = [value], [value]
    for step in range(half):
        behind.append(along_z(behind[-1], 1))
        if step < half - 1:
            ahead.append(along_z(ahead[-1], -1))
    return behind + ahead[:0:-1]


def picker(blocks, axis, home):
    count = blocks.shape[axis]
    return lambda steps: lax.dynamic_index_in_dim(
        blocks, (home + steps) % count, axis, keepdims=False
    )


def add(*terms):
    total = terms[0].astype(jnp.float32)
    for term in terms[1:]:
        total = total + term.astype(jnp.float32)
    return total


def collect(blocks, home, along):
    block = picker(blocks, 0, home)
    return add(block(0), *[along(block(steps), steps) for steps in range(1, blocks.shape[0])])


def reduce_x(blocks, axis, home):
    block = picker(blocks, axis, home)
    far, behind, ahead = block(2), block(1), block(-1)
    half = far.shape[0] // 2
    from_behind, from_ahead = along_x(far[:half], 1), along_x(far[half:], -1)
    behind = jnp.concatenate([add(behind[:half], from_behind).astype(jnp.bfloat16), behind[half:]])
    ahead = jnp.concatenate([ahead[:half], add(ahead[half:], from_ahead).astype(jnp.bfloat16)])
    return add(block(0), along_x(behind, 1), along_x(ahead, -1))


def reduce_z(blocks, axis, home):
    block = picker(blocks, axis, home)
    half = Z_SIZE // 2
    behind, ahead = block(half), block(1 - half)
    for steps in range(half - 1, 0, -1):
        behind = add(along_z(behind, 1), block(steps)).astype(jnp.bfloat16)
        if steps < half - 1:
            ahead = add(along_z(ahead, -1), block(-steps)).astype(jnp.bfloat16)
    return add(block(0), along_z(behind, 1), along_z(ahead, -1))


def all_sum(value, axis):
    count = lax.axis_size(axis)
    step = 1
    while step < count:
        value = value + lax.ppermute(value, axis, [(place, place ^ step) for place in range(count)])
        step *= 2
    return value


def outer_sum(left, right):
    return lax.dot_general(
        left, right, (((0, 1), (0, 1)), ((), ())), preferred_element_type=jnp.float32
    )


def body(crop_maps, target_maps, crop_counts, depth_kernels, weight_in, weight_out, head_weight):
    section = lax.axis_index("section")
    sections = lax.axis_size("section")
    stages = sections // BLOCKS
    stage = section // BLOCKS
    core = section % BLOCKS
    micros, slots = crop_maps.shape[1:3]
    width = crop_maps.shape[-1]
    cells = SIDE * SIDE
    other = [(index, index ^ 1) for index in range(sections)]
    onward = [(index, index + BLOCKS) for index in range(sections - BLOCKS)]
    back = [(index + BLOCKS, index) for index in range(sections - BLOCKS)]

    group = lax.axis_index("dp")
    home_z, home_x = group // X_SIZE, group % X_SIZE
    home = jnp.stack([home_z, home_x]).astype(jnp.int32)
    shard_rows, expand = weight_in.shape[1:]
    first_shard = weight_in[0].reshape(shard_rows // 2, 2, expand)
    far_z, far_x = range(Z_SIZE), range(X_SIZE)
    second_column = jnp.stack(spread_z(weight_out[0]))
    first_pieces = chain_z(jnp.stack(spread_x(first_shard)))
    first_places = [[(z, x) for x in far_x] for z in far_z]
    second_pieces = chain_x(second_column)
    ordered = [[(z, x) for z in far_z] for x in far_x]
    second_places = ordered[:2] + [ordered[2][: Z_SIZE // 2], ordered[2][Z_SIZE // 2 :]] + ordered[3:]
    own_out = assemble(home, second_pieces, second_places).reshape(expand, width)
    own_in = assemble(home, first_pieces, first_places).reshape(width, expand)
    other_in = lax.ppermute(own_in, "section", other)
    other_out = lax.ppermute(own_out, "section", other)
    weights = (own_in, other_in, own_out, other_out)
    other_kernel = lax.ppermute(depth_kernels[0], "section", other)
    first_kernel = jnp.where(core == 0, depth_kernels[0], other_kernel)
    second_kernel = jnp.where(core == 0, other_kernel, depth_kernels[0])
    kernels = jnp.stack([first_kernel, second_kernel])

    crops = micros * slots // BLOCKS
    steps = crops // STEP_CROPS
    step_cells = STEP_CROPS * cells
    live = (jnp.arange(slots)[None, :] < crop_counts[0][:, None]).reshape(crops, BLOCKS)
    pick = lambda value: lax.dynamic_index_in_dim(value, core, 1, keepdims=False)
    own_live = pick(live).astype(jnp.float32)[:, None]
    own_crops = pick(crop_maps[0].reshape(crops, BLOCKS, cells, width))
    own_targets = pick(target_maps[0].reshape(crops, BLOCKS, cells))
    entering = own_crops * own_live[:, :, None].astype(jnp.bfloat16)
    entering = entering.reshape(steps, step_cells, width)

    ticks = steps + stages - 1
    spare = steps

    def kept(*tail, dtype):
        return jax.ShapeDtypeStruct((BLOCKS, steps + 1, step_cells) + tail, dtype)

    tile_shape = jax.ShapeDtypeStruct((step_cells, width), jnp.bfloat16)
    forward_shapes = [
        kept(width, dtype=jnp.bfloat16),
        kept(width, dtype=jnp.bfloat16),
        kept(LANES, dtype=jnp.float32),
        kept(expand, dtype=jnp.bfloat16),
        kept(expand, dtype=jnp.bfloat16),
    ]
    saved = None
    arrived = entering[0]
    finals = []
    for moment in range(ticks):
        micro = moment - stage
        place = jnp.where((micro >= 0) & (micro < steps), micro, spare)
        control = jnp.stack([place, core, stage == 0]).astype(jnp.int32)
        result, saved = call_stage(
            forward_kernel, "forward", control,
            [entering[min(moment, steps - 1)], arrived, kernels], [], weights,
            saved, forward_shapes, tile_shape,
        )
        if moment >= stages - 1:
            finals.append(result)
        if moment < ticks - 1:
            arrived = lax.ppermute(result, "section", onward)
    inputs, lows, inverse, slope, active = saved

    is_last = stage == stages - 1
    by_cell = lambda value: value.reshape(crops * cells, 1).astype(jnp.float32)
    seeds = pl.pallas_call(
        head_kernel,
        name="head",
        out_shape=jax.ShapeDtypeStruct((steps, step_cells + RIDERS, width), jnp.bfloat16),
        compiler_params=pltpu.CompilerParams(vmem_limit_bytes=SMALL_LIMIT),
    )(
        *finals,
        by_cell(own_targets),
        by_cell(jnp.broadcast_to(own_live, own_targets.shape)),
        head_weight[None],
    )

    backward_shapes = [
        kept(width, dtype=jnp.bfloat16),
        kept(expand, dtype=jnp.bfloat16),
        kept(width, dtype=jnp.float32),
    ]
    upstream_shape = jax.ShapeDtypeStruct((step_cells + RIDERS, width), jnp.bfloat16)
    grads = None
    arrived = seeds[0]
    for moment in range(ticks):
        micro = moment - (stages - 1 - stage)
        place = jnp.where((micro >= 0) & (micro < steps), micro, spare)
        control = jnp.stack([place, core, is_last]).astype(jnp.int32)
        result, grads = call_stage(
            backward_kernel, "backward", control,
            [seeds[min(moment, steps - 1)], arrived, kernels],
            [lows, inverse, slope], weights, grads, backward_shapes, upstream_shape,
        )
        if moment < ticks - 1:
            arrived = lax.ppermute(result, "section", back)
    ups, hidden_grads, mixed_grads = grads

    def block_of(value, which):
        return lax.dynamic_index_in_dim(value, which, 0, keepdims=False)[:steps]

    def outer_pair(which):
        return (
            outer_sum(block_of(lows, which), block_of(hidden_grads, which)),
            outer_sum(block_of(active, which), block_of(ups, which)),
        )

    away_in, away_out = (value.astype(jnp.bfloat16) for value in outer_pair(1 - core))
    came_in = lax.ppermute(away_in, "section", other)
    came_out = lax.ppermute(away_out, "section", other)
    home_in, home_out = outer_pair(core)
    by_group = lambda value, *tail: value.astype(jnp.bfloat16).reshape((Z_SIZE, X_SIZE) + tail)
    sum_out = by_group(home_out + came_out.astype(jnp.float32), expand // Z_SIZE // X_SIZE, width)
    sum_in = by_group(home_in + came_in.astype(jnp.float32), *first_shard.shape)

    taps = tap_grads(inputs, mixed_grads)
    riders = result[step_cells : step_cells + 4].astype(jnp.float32)
    riders = jnp.stack([riders[0] + riders[1], riders[2] + riders[3]])
    tap_of = lambda which: jnp.concatenate(
        [lax.dynamic_index_in_dim(taps, which, 0, keepdims=False), riders]
    )
    small = tap_of(core) + lax.ppermute(tap_of(1 - core), "section", other)
    small, sum_in, sum_out = lax.optimization_barrier((small, sum_in, sum_out))

    second_part = reduce_z(sum_out, 0, home_z).astype(jnp.bfloat16)
    first_part = reduce_x(sum_in, 1, home_x).astype(jnp.bfloat16)
    second_part = collect(second_part, home_x, along_x)
    first_part = collect(first_part, home_z, along_z).reshape(shard_rows, expand)
    small = all_sum(small, "dp")
    tap_count = TAPS * TAPS
    return (
        first_part[None],
        second_part[None],
        small[None, :tap_count],
        small[tap_count],
        small[tap_count + 1, 0],
    )


def solution(mesh):
    return jax.shard_map(
        body,
        mesh=mesh,
        in_specs=(
            P("dp", None, None, None, None, None),
            P("dp", None, None, None, None),
            P("dp", None),
            P("section", None, None),
            P("section", "dp", None),
            P("section", "dp", None),
            P(),
        ),
        out_specs=(
            P("section", "dp", None),
            P("section", "dp", None),
            P("section", None, None),
            P(),
            P(),
        ),
        check_vma=False,
    )
```

```python
import jax
import jax.numpy as jnp
from jax import lax
from jax.experimental import pallas as pl
from jax.experimental.pallas import tpu as pltpu
from jax.sharding import PartitionSpec as P

EPSILON = 1e-06
SQRT_HALF = 0.7071067811865476
INV_ROOT_TWO_PI = 0.3989422804014327
SIDE = 8
REACH = 3
TAPS = 7
LANES = 128
Z_SIZE = 8
X_SIZE = 4
BLOCKS = 2
STEP_CROPS = 2
CHUNK = 1280
RIDERS = 16
FORWARD_KEPT = 5
BACKWARD_KEPT = 3
VMEM_LIMIT = 24 * 1024 * 1024
SMALL_LIMIT = 8 * 1024 * 1024


def shifted(rows, offset):
    if offset == 0:
        return rows
    place = lax.broadcasted_iota(jnp.int32, rows.shape, 0) + offset
    moved = pltpu.roll(rows, (-offset) % SIDE, 0)
    return jnp.where((place >= 0) & (place < SIDE), moved, 0.0)


def depthwise_into(source, kernel, target, backward):
    cells, width = source.shape
    sign = -1 if backward else 1
    for start in range(0, cells, SIDE * SIDE):
        for first in range(0, width, LANES):
            lanes = pl.ds(first, LANES)
            rows = [source[pl.ds(start + y * SIDE, SIDE), lanes] for y in range(SIDE)]
            sums = [None] * SIDE
            for across in range(TAPS):
                moved = [shifted(row, sign * (across - REACH)) for row in rows]
                for vertical in range(TAPS):
                    tap = kernel[pl.ds(vertical * TAPS + across, 1), lanes]
                    for y in range(SIDE):
                        origin = y + sign * (vertical - REACH)
                        if 0 <= origin < SIDE:
                            term = moved[origin] * tap
                            sums[y] = term if sums[y] is None else sums[y] + term
            for y in range(SIDE):
                target[pl.ds(start + y * SIDE, SIDE), lanes] = sums[y]


def fetch(control, block, own, other, buffer, semaphore):
    @pl.when(control[1] == block)
    def _():
        pltpu.make_async_copy(own, buffer.at[block], semaphore).start()

    @pl.when(control[1] != block)
    def _():
        pltpu.make_async_copy(other, buffer.at[block], semaphore).start()

    return pltpu.make_async_copy(own, buffer.at[block], semaphore)


def begin(control, own_tiles, arrived, kernels, incoming, taps, ready):
    @pl.when(control[2] == 1)
    def _():
        pltpu.make_async_copy(own_tiles, incoming, ready.at[0]).start()

    @pl.when(control[2] != 1)
    def _():
        pltpu.make_async_copy(arrived, incoming, ready.at[0]).start()

    taps_copy = pltpu.make_async_copy(kernels, taps, ready.at[1])
    taps_copy.start()
    return pltpu.make_async_copy(own_tiles, incoming, ready.at[0]), taps_copy


def forward_kernel(
    control, own_tiles, arrived, kernels, own_in, other_in, own_out, other_out, *rest
):
    rest = rest[-(1 + FORWARD_KEPT * 2 + 9):]
    result, rest = rest[0], rest[1:]
    kept_out, rest = rest[:FORWARD_KEPT], rest[FORWARD_KEPT:]
    kept, rest = rest[:FORWARD_KEPT], rest[FORWARD_KEPT:]
    first_buffer, second_buffer, weight_ready, kept_done, wide, mixed = rest[:6]
    incoming, taps, ready = rest[6:]
    inputs, lows, inverses, slopes, actives = kept
    expand = own_in.shape[1]
    tiles_copy, taps_copy = begin(control, own_tiles, arrived, kernels, incoming, taps, ready)
    loads = []
    for block in range(BLOCKS):
        loads.append(
            (
                fetch(control, block, own_in, other_in, first_buffer, weight_ready.at[block, 0]),
                fetch(control, block, own_out, other_out, second_buffer, weight_ready.at[block, 1]),
            )
        )
    stores = []
    tiles_copy.wait()
    wide[...] = incoming[...].astype(jnp.float32)
    taps_copy.wait()
    for block in range(BLOCKS):
        inputs[block] = wide[...].astype(jnp.bfloat16)
        depthwise_into(wide, taps.at[block], mixed, False)
        values = mixed[...]
        centred = values - jnp.mean(values, axis=-1, keepdims=True)
        inverse = lax.rsqrt(jnp.mean(centred * centred, axis=-1, keepdims=True) + EPSILON)
        inverses[block] = jnp.broadcast_to(inverse, inverses.shape[1:])
        low = (centred * inverse).astype(jnp.bfloat16)
        lows[block] = low
        loads[block][0].wait()
        total = jnp.zeros(wide.shape, jnp.float32)
        for start in range(0, expand, CHUNK):
            part = slice(start, start + CHUNK)
            hidden = jnp.dot(low, first_buffer[block, :, part], preferred_element_type=jnp.float32)
            half = 0.5 * (1.0 + lax.erf(hidden * SQRT_HALF))
            active = (hidden * half).astype(jnp.bfloat16)
            slope = half + hidden * jnp.exp(-0.5 * hidden * hidden) * INV_ROOT_TWO_PI
            slopes[block, :, part] = slope.astype(jnp.bfloat16)
            actives[block, :, part] = active
            if start == 0:
                loads[block][1].wait()
            total = total + jnp.dot(
                active, second_buffer[block, part, :], preferred_element_type=jnp.float32
            )
        wide[...] = (wide[...] + total).astype(jnp.bfloat16).astype(jnp.float32)
        for index in range(FORWARD_KEPT):
            copy = pltpu.make_async_copy(
                kept[index].at[block], kept_out[index].at[block, control[0]], kept_done.at[block, index]
            )
            copy.start()
            stores.append(copy)
    result[...] = wide[...].astype(jnp.bfloat16)
    for copy in stores:
        copy.wait()


def backward_kernel(
    control, seeds, arrived, kernels, lows_all, inverses_all, slopes_all,
    own_in, other_in, own_out, other_out, *rest
):
    rest = rest[-(1 + BACKWARD_KEPT * 2 + 13):]
    result, rest = rest[0], rest[1:]
    kept_out, rest = rest[:BACKWARD_KEPT], rest[BACKWARD_KEPT:]
    kept, rest = rest[:BACKWARD_KEPT], rest[BACKWARD_KEPT:]
    lows, inverses, slopes, known_ready = rest[:4]
    first_buffer, second_buffer, weight_ready, kept_done, wide, spread = rest[4:10]
    incoming, taps, ready = rest[10:]
    ups, hiddens, mixeds = kept
    expand = own_in.shape[1]
    tiles_copy, taps_copy = begin(control, seeds, arrived, kernels, incoming, taps, ready)
    loads = [None] * BLOCKS
    for block in range(BLOCKS - 1, -1, -1):
        second = fetch(control, block, own_out, other_out, second_buffer, weight_ready.at[block, 1])
        known = []
        for index, (source, target) in enumerate(
            ((slopes_all, slopes), (lows_all, lows), (inverses_all, inverses))
        ):
            copy = pltpu.make_async_copy(
                source.at[block, control[0]], target.at[block], known_ready.at[block, index]
            )
            copy.start()
            known.append(copy)
        first = fetch(control, block, own_in, other_in, first_buffer, weight_ready.at[block, 0])
        loads[block] = (second, known, first)
    stores = []
    across = (((1,), (1,)), ((), ()))
    cells = wide.shape[0]
    tiles_copy.wait()
    wide[...] = incoming[:cells, :].astype(jnp.float32)
    taps_copy.wait()
    for block in range(BLOCKS - 1, -1, -1):
        second, known, first = loads[block]
        low = wide[...].astype(jnp.bfloat16)
        ups[block] = low
        total = jnp.zeros(wide.shape, jnp.float32)
        second.wait()
        for copy in known:
            copy.wait()
        for start in range(0, expand, CHUNK):
            part = slice(start, start + CHUNK)
            through = lax.dot_general(
                low, second_buffer[block, part, :], across, preferred_element_type=jnp.float32
            )
            grads = (through * slopes[block, :, part].astype(jnp.float32)).astype(jnp.bfloat16)
            hiddens[block, :, part] = grads
            if start == 0:
                first.wait()
            total = total + lax.dot_general(
                grads, first_buffer[block, :, part], across, preferred_element_type=jnp.float32
            )
        normed = lows[block].astype(jnp.float32)
        mixeds[block] = inverses[block][:, :1] * (
            total
            - jnp.mean(total, axis=-1, keepdims=True)
            - normed * jnp.mean(total * normed, axis=-1, keepdims=True)
        )
        depthwise_into(mixeds.at[block], taps.at[block], spread, True)
        wide[...] = (wide[...] + spread[...]).astype(jnp.bfloat16).astype(jnp.float32)
        for index in range(BACKWARD_KEPT):
            copy = pltpu.make_async_copy(
                kept[index].at[block], kept_out[index].at[block, control[0]], kept_done.at[block, index]
            )
            copy.start()
            stores.append(copy)
    result[:cells, :] = wide[...].astype(jnp.bfloat16)
    result[cells:, :] = incoming[cells:, :]
    for copy in stores:
        copy.wait()


def taps_kernel(inputs, mixed, result):
    steps, cells = inputs.shape[1:3]
    tile = SIDE * SIDE
    for across in range(TAPS):
        sums = [None] * TAPS
        for step in range(steps):
            for start in range(0, cells, tile):
                strips = [pl.ds(start + y * SIDE, SIDE) for y in range(SIDE)]
                rows = [inputs[0, step, strip, :].astype(jnp.float32) for strip in strips]
                moved = [shifted(mixed[0, step, strip, :], REACH - across) for strip in strips]
                for vertical in range(TAPS):
                    for y in range(SIDE):
                        origin = y - (vertical - REACH)
                        if 0 <= origin < SIDE:
                            term = rows[y] * moved[origin]
                            known = sums[vertical]
                            sums[vertical] = term if known is None else known + term
        for vertical in range(TAPS):
            result[0, pl.ds(vertical * TAPS + across, 1), :] = jnp.sum(
                sums[vertical], axis=0, keepdims=True
            )


def call_stage(kernel, name, control, fixed, known, weights, saved, saved_shapes, out_shape):
    scalar = pl.BlockSpec(memory_space=pltpu.SMEM)
    near = pl.BlockSpec(memory_space=pltpu.VMEM)
    far = pl.BlockSpec(memory_space=pl.ANY)
    at_home = lambda value: pltpu.with_memory_space_constraint(value, pltpu.HBM)
    operands = [control, *fixed[:2], *[at_home(value) for value in (*fixed[2:], *known, *weights)]]
    in_specs = [scalar] + [far] * (len(fixed) + len(known) + len(weights))
    aliases = {}
    if saved is not None:
        for index, value in enumerate(saved):
            aliases[len(operands)] = 1 + index
            operands.append(at_home(value))
            in_specs.append(far)

    def buffer(value):
        return pltpu.VMEM((BLOCKS,) + value.shape[2:], value.dtype)

    scratch = [buffer(value) for value in saved_shapes]
    if known:
        lows, inverses, slopes = known
        scratch += [buffer(lows), buffer(inverses), buffer(slopes)]
        scratch += [pltpu.SemaphoreType.DMA((BLOCKS, len(known)))]
    scratch += [
        pltpu.VMEM((BLOCKS,) + weights[0].shape, weights[0].dtype),
        pltpu.VMEM((BLOCKS,) + weights[2].shape, weights[2].dtype),
        pltpu.SemaphoreType.DMA((BLOCKS, 2)),
        pltpu.SemaphoreType.DMA((BLOCKS, len(saved_shapes))),
        pltpu.VMEM((saved_shapes[0].shape[2], out_shape.shape[1]), jnp.float32),
        pltpu.VMEM((saved_shapes[0].shape[2], out_shape.shape[1]), jnp.float32),
        pltpu.VMEM(fixed[0].shape, fixed[0].dtype),
        pltpu.VMEM(fixed[2].shape, fixed[2].dtype),
        pltpu.SemaphoreType.DMA((2,)),
    ]
    outputs = pl.pallas_call(
        kernel,
        name=name,
        out_shape=[out_shape, *[pltpu.HBM(value.shape, value.dtype) for value in saved_shapes]],
        in_specs=in_specs,
        out_specs=[near] + [far] * len(saved_shapes),
        scratch_shapes=scratch,
        input_output_aliases=aliases,
        compiler_params=pltpu.CompilerParams(vmem_limit_bytes=VMEM_LIMIT),
    )(*operands)
    return outputs[0], tuple(outputs[1:])


def tap_grads(inputs, mixed):
    blocks, crops, cells, width = inputs.shape
    window = pl.BlockSpec((1, crops - 1, cells, LANES), lambda block, lane: (block, 0, 0, lane))
    return pl.pallas_call(
        taps_kernel,
        name="taps",
        out_shape=jax.ShapeDtypeStruct((blocks, TAPS * TAPS, width), jnp.float32),
        grid=(blocks, width // LANES),
        in_specs=[window, window],
        out_specs=pl.BlockSpec((1, TAPS * TAPS, LANES), lambda block, lane: (block, 0, lane)),
        compiler_params=pltpu.CompilerParams(vmem_limit_bytes=SMALL_LIMIT),
    )(inputs, mixed)


def head_kernel(*refs):
    finals, (truth, live, weight, seeds) = refs[:-4], refs[-4:]
    step_cells = finals[0].shape[0]
    factor = SIDE * SIDE / (BLOCKS * len(finals) * step_cells)
    head_term = jnp.zeros(weight.shape, jnp.float32)
    loss_term = jnp.zeros((1, 1), jnp.float32)
    for crop, final in enumerate(finals):
        cells = pl.ds(crop * step_cells, step_cells)
        widened = final[...].astype(jnp.float32)
        logits = jnp.sum(widened * weight[...], axis=-1, keepdims=True)
        softplus = jnp.maximum(logits, 0.0) + jnp.log1p(jnp.exp(-jnp.abs(logits)))
        loss = live[cells, :] * (softplus - truth[cells, :] * logits)
        loss_term = loss_term + jnp.sum(loss, axis=0, keepdims=True) * factor
        grads = (jax.nn.sigmoid(logits) - truth[cells, :]) * live[cells, :] * factor
        seeds[crop, :step_cells, :] = (grads * weight[...]).astype(jnp.bfloat16)
        head_term = head_term + jnp.sum(grads * widened, axis=0, keepdims=True)
    place = lax.broadcasted_iota(jnp.int32, (RIDERS, weight.shape[1]), 0)
    riders = jnp.where(place < 2, head_term, jnp.where(place < 4, loss_term, 0.0))
    coarse = riders.astype(jnp.bfloat16)
    rest = (riders - coarse.astype(jnp.float32)).astype(jnp.bfloat16)
    riders = jnp.where(place % 2 == 0, coarse, rest)
    for crop in range(len(finals)):
        seeds[crop, step_cells:, :] = riders


def assemble(control, pieces, distances):
    def kernel(control, *refs):
        sources, result, ready = refs[:-2], refs[-2], refs[-1]
        copies = []
        for source, shards in zip(sources, distances):
            for index, (z_steps, x_steps) in enumerate(shards):
                target = (control[0] - z_steps) % Z_SIZE * X_SIZE + (control[1] - x_steps) % X_SIZE
                copy = pltpu.make_async_copy(
                    source.at[index], result.at[target], ready.at[len(copies)]
                )
                copy.start()
                copies.append(copy)
        for copy in copies:
            copy.wait()

    piece = pieces[0]
    far = pl.BlockSpec(memory_space=pl.ANY)
    return pl.pallas_call(
        kernel,
        name="assemble",
        out_shape=pltpu.HBM((Z_SIZE * X_SIZE,) + piece.shape[1:], piece.dtype),
        in_specs=[pl.BlockSpec(memory_space=pltpu.SMEM)] + [far] * len(pieces),
        out_specs=far,
        scratch_shapes=[pltpu.SemaphoreType.DMA((Z_SIZE * X_SIZE,))],
        compiler_params=pltpu.CompilerParams(vmem_limit_bytes=SMALL_LIMIT),
    )(control, *[pltpu.with_memory_space_constraint(piece, pltpu.HBM) for piece in pieces])


def along_x(value, steps):
    pairs = [
        (z * X_SIZE + x, z * X_SIZE + (x + steps) % X_SIZE)
        for z in range(Z_SIZE)
        for x in range(X_SIZE)
    ]
    return lax.ppermute(value, "dp", pairs)


def along_z(value, steps):
    pairs = [
        (z * X_SIZE + x, (z + steps) % Z_SIZE * X_SIZE + x)
        for z in range(Z_SIZE)
        for x in range(X_SIZE)
    ]
    return lax.ppermute(value, "dp", pairs)


def spread_x(value):
    return [value] + [along_x(value, steps) for steps in range(1, X_SIZE)]


def spread_z(value):
    return [value] + [along_z(value, steps) for steps in range(1, Z_SIZE)]


def chain_x(value):
    half = value.shape[0] // 2
    behind, ahead = along_x(value, 1), along_x(value, -1)
    return [value, behind, along_x(behind[:half], 1), along_x(ahead[half:], -1), ahead]


def chain_z(value):
    half = Z_SIZE // 2
    behind, ahead = [value], [value]
    for step in range(half):
        behind.append(along_z(behind[-1], 1))
        if step < half - 1:
            ahead.append(along_z(ahead[-1], -1))
    return behind + ahead[:0:-1]


def picker(blocks, axis, home):
    count = blocks.shape[axis]
    return lambda steps: lax.dynamic_index_in_dim(
        blocks, (home + steps) % count, axis, keepdims=False
    )


def add(*terms):
    total = terms[0].astype(jnp.float32)
    for term in terms[1:]:
        total = total + term.astype(jnp.float32)
    return total


def collect(blocks, home, along):
    block = picker(blocks, 0, home)
    return add(block(0), *[along(block(steps), steps) for steps in range(1, blocks.shape[0])])


def reduce_x(blocks, axis, home):
    block = picker(blocks, axis, home)
    far, behind, ahead = block(2), block(1), block(-1)
    half = far.shape[0] // 2
    from_behind, from_ahead = along_x(far[:half], 1), along_x(far[half:], -1)
    behind = jnp.concatenate([add(behind[:half], from_behind).astype(jnp.bfloat16), behind[half:]])
    ahead = jnp.concatenate([ahead[:half], add(ahead[half:], from_ahead).astype(jnp.bfloat16)])
    return add(block(0), along_x(behind, 1), along_x(ahead, -1))


def reduce_z(blocks, axis, home):
    block = picker(blocks, axis, home)
    half = Z_SIZE // 2
    behind, ahead = block(half), block(1 - half)
    for steps in range(half - 1, 0, -1):
        behind = add(along_z(behind, 1), block(steps)).astype(jnp.bfloat16)
        if steps < half - 1:
            ahead = add(along_z(ahead, -1), block(-steps)).astype(jnp.bfloat16)
    return add(block(0), along_z(behind, 1), along_z(ahead, -1))


def all_sum(value, axis):
    count = lax.axis_size(axis)
    step = 1
    while step < count:
        value = value + lax.ppermute(value, axis, [(place, place ^ step) for place in range(count)])
        step *= 2
    return value


def outer_sum(left, right):
    return lax.dot_general(
        left, right, (((0, 1), (0, 1)), ((), ())), preferred_element_type=jnp.float32
    )


def body(crop_maps, target_maps, crop_counts, depth_kernels, weight_in, weight_out, head_weight):
    section = lax.axis_index("section")
    sections = lax.axis_size("section")
    stages = sections // BLOCKS
    stage = section // BLOCKS
    core = section % BLOCKS
    micros, slots = crop_maps.shape[1:3]
    width = crop_maps.shape[-1]
    cells = SIDE * SIDE
    other = [(index, index ^ 1) for index in range(sections)]
    onward = [(index, index + BLOCKS) for index in range(sections - BLOCKS)]
    back = [(index + BLOCKS, index) for index in range(sections - BLOCKS)]

    group = lax.axis_index("dp")
    home_z, home_x = group // X_SIZE, group % X_SIZE
    home = jnp.stack([home_z, home_x]).astype(jnp.int32)
    shard_rows, expand = weight_in.shape[1:]
    first_shard = weight_in[0].reshape(shard_rows // 2, 2, expand)
    far_z, far_x = range(Z_SIZE), range(X_SIZE)
    second_column = jnp.stack(spread_z(weight_out[0]))
    first_pieces = chain_z(jnp.stack(spread_x(first_shard)))
    first_places = [[(z, x) for x in far_x] for z in far_z]
    second_pieces = chain_x(second_column)
    ordered = [[(z, x) for z in far_z] for x in far_x]
    second_places = ordered[:2] + [ordered[2][: Z_SIZE // 2], ordered[2][Z_SIZE // 2 :]] + ordered[3:]
    own_out = assemble(home, second_pieces, second_places).reshape(expand, width)
    own_in = assemble(home, first_pieces, first_places).reshape(width, expand)
    other_in = lax.ppermute(own_in, "section", other)
    other_out = lax.ppermute(own_out, "section", other)
    weights = (own_in, other_in, own_out, other_out)
    other_kernel = lax.ppermute(depth_kernels[0], "section", other)
    first_kernel = jnp.where(core == 0, depth_kernels[0], other_kernel)
    second_kernel = jnp.where(core == 0, other_kernel, depth_kernels[0])
    kernels = jnp.stack([first_kernel, second_kernel])

    crops = micros * slots // BLOCKS
    steps = crops // STEP_CROPS
    step_cells = STEP_CROPS * cells
    live = (jnp.arange(slots)[None, :] < crop_counts[0][:, None]).reshape(crops, BLOCKS)
    pick = lambda value: lax.dynamic_index_in_dim(value, core, 1, keepdims=False)
    own_live = pick(live).astype(jnp.float32)[:, None]
    own_crops = pick(crop_maps[0].reshape(crops, BLOCKS, cells, width))
    own_targets = pick(target_maps[0].reshape(crops, BLOCKS, cells))
    entering = own_crops * own_live[:, :, None].astype(jnp.bfloat16)
    entering = entering.reshape(steps, step_cells, width)

    ticks = steps + stages - 1
    spare = steps

    def kept(*tail, dtype):
        return jax.ShapeDtypeStruct((BLOCKS, steps + 1, step_cells) + tail, dtype)

    tile_shape = jax.ShapeDtypeStruct((step_cells, width), jnp.bfloat16)
    forward_shapes = [
        kept(width, dtype=jnp.bfloat16),
        kept(width, dtype=jnp.bfloat16),
        kept(LANES, dtype=jnp.float32),
        kept(expand, dtype=jnp.bfloat16),
        kept(expand, dtype=jnp.bfloat16),
    ]
    saved = None
    arrived = entering[0]
    finals = []
    for moment in range(ticks):
        micro = moment - stage
        place = jnp.where((micro >= 0) & (micro < steps), micro, spare)
        control = jnp.stack([place, core, stage == 0]).astype(jnp.int32)
        result, saved = call_stage(
            forward_kernel, "forward", control,
            [entering[min(moment, steps - 1)], arrived, kernels], [], weights,
            saved, forward_shapes, tile_shape,
        )
        if moment >= stages - 1:
            finals.append(result)
        if moment < ticks - 1:
            arrived = lax.ppermute(result, "section", onward)
    inputs, lows, inverse, slope, active = saved

    is_last = stage == stages - 1
    by_cell = lambda value: value.reshape(crops * cells, 1).astype(jnp.float32)
    seeds = pl.pallas_call(
        head_kernel,
        name="head",
        out_shape=jax.ShapeDtypeStruct((steps, step_cells + RIDERS, width), jnp.bfloat16),
        compiler_params=pltpu.CompilerParams(vmem_limit_bytes=SMALL_LIMIT),
    )(
        *finals,
        by_cell(own_targets),
        by_cell(jnp.broadcast_to(own_live, own_targets.shape)),
        head_weight[None],
    )

    backward_shapes = [
        kept(width, dtype=jnp.bfloat16),
        kept(expand, dtype=jnp.bfloat16),
        kept(width, dtype=jnp.float32),
    ]
    upstream_shape = jax.ShapeDtypeStruct((step_cells + RIDERS, width), jnp.bfloat16)
    grads = None
    arrived = seeds[0]
    for moment in range(ticks):
        micro = moment - (stages - 1 - stage)
        place = jnp.where((micro >= 0) & (micro < steps), micro, spare)
        control = jnp.stack([place, core, is_last]).astype(jnp.int32)
        result, grads = call_stage(
            backward_kernel, "backward", control,
            [seeds[min(moment, steps - 1)], arrived, kernels],
            [lows, inverse, slope], weights, grads, backward_shapes, upstream_shape,
        )
        if moment < ticks - 1:
            arrived = lax.ppermute(result, "section", back)
    ups, hidden_grads, mixed_grads = grads

    taps = tap_grads(inputs, mixed_grads)
    riders = result[step_cells : step_cells + 4].astype(jnp.float32)
    riders = jnp.stack([riders[0] + riders[1], riders[2] + riders[3]])
    tap_of = lambda which: jnp.concatenate(
        [lax.dynamic_index_in_dim(taps, which, 0, keepdims=False), riders]
    )
    small_home, small_away, hidden_grads, ups = lax.optimization_barrier(
        (tap_of(core), tap_of(1 - core), hidden_grads, ups)
    )
    small = all_sum(small_home + lax.ppermute(small_away, "section", other), "dp")

    def block_of(value, which):
        return lax.dynamic_index_in_dim(value, which, 0, keepdims=False)[:steps]

    def outer_in(which):
        return outer_sum(block_of(lows, which), block_of(hidden_grads, which))

    def outer_out(which):
        return outer_sum(block_of(active, which), block_of(ups, which))

    came_out = lax.ppermute(outer_out(1 - core).astype(jnp.bfloat16), "section", other)
    came_in = lax.ppermute(outer_in(1 - core).astype(jnp.bfloat16), "section", other)
    by_group = lambda value, *tail: value.astype(jnp.bfloat16).reshape((Z_SIZE, X_SIZE) + tail)
    sum_out = outer_out(core) + came_out.astype(jnp.float32)
    sum_out = by_group(sum_out, expand // Z_SIZE // X_SIZE, width)
    sum_in = by_group(outer_in(core) + came_in.astype(jnp.float32), *first_shard.shape)
    small, sum_in, sum_out = lax.optimization_barrier((small, sum_in, sum_out))

    second_part = reduce_z(sum_out, 0, home_z).astype(jnp.bfloat16)
    first_part = reduce_x(sum_in, 1, home_x).astype(jnp.bfloat16)
    second_part = collect(second_part, home_x, along_x)
    first_part = collect(first_part, home_z, along_z).reshape(shard_rows, expand)
    tap_count = TAPS * TAPS
    return (
        first_part[None],
        second_part[None],
        small[None, :tap_count],
        small[tap_count],
        small[tap_count + 1, 0],
    )


def solution(mesh):
    return jax.shard_map(
        body,
        mesh=mesh,
        in_specs=(
            P("dp", None, None, None, None, None),
            P("dp", None, None, None, None),
            P("dp", None),
            P("section", None, None),
            P("section", "dp", None),
            P("section", "dp", None),
            P(),
        ),
        out_specs=(
            P("section", "dp", None),
            P("section", "dp", None),
            P("section", None, None),
            P(),
            P(),
        ),
        check_vma=False,
    )
```

```python
import jax
import jax.numpy as jnp
from jax import lax
from jax.experimental import pallas as pl
from jax.experimental.pallas import tpu as pltpu
from jax.sharding import PartitionSpec as P

EPSILON = 1e-06
SQRT_HALF = 0.7071067811865476
INV_ROOT_TWO_PI = 0.3989422804014327
SIDE = 8
REACH = 3
TAPS = 7
LANES = 128
Z_SIZE = 8
X_SIZE = 4
BLOCKS = 2
STEP_CROPS = 2
CHUNK = 1280
RIDERS = 16
FORWARD_KEPT = 5
BACKWARD_KEPT = 3
VMEM_LIMIT = 24 * 1024 * 1024
SMALL_LIMIT = 8 * 1024 * 1024


def shifted(rows, offset):
    if offset == 0:
        return rows
    place = lax.broadcasted_iota(jnp.int32, rows.shape, 0) + offset
    moved = pltpu.roll(rows, (-offset) % SIDE, 0)
    return jnp.where((place >= 0) & (place < SIDE), moved, 0.0)


def depthwise_into(source, kernel, target, backward):
    cells, width = source.shape
    sign = -1 if backward else 1
    for start in range(0, cells, SIDE * SIDE):
        for first in range(0, width, LANES):
            lanes = pl.ds(first, LANES)
            rows = [source[pl.ds(start + y * SIDE, SIDE), lanes] for y in range(SIDE)]
            sums = [None] * SIDE
            for across in range(TAPS):
                moved = [shifted(row, sign * (across - REACH)) for row in rows]
                for vertical in range(TAPS):
                    tap = kernel[pl.ds(vertical * TAPS + across, 1), lanes]
                    for y in range(SIDE):
                        origin = y + sign * (vertical - REACH)
                        if 0 <= origin < SIDE:
                            term = moved[origin] * tap
                            sums[y] = term if sums[y] is None else sums[y] + term
            for y in range(SIDE):
                target[pl.ds(start + y * SIDE, SIDE), lanes] = sums[y]


def fetch(control, block, own, other, buffer, semaphore):
    @pl.when(control[1] == block)
    def _():
        pltpu.make_async_copy(own, buffer.at[block], semaphore).start()

    @pl.when(control[1] != block)
    def _():
        pltpu.make_async_copy(other, buffer.at[block], semaphore).start()

    return pltpu.make_async_copy(own, buffer.at[block], semaphore)


def begin(control, own_tiles, arrived, kernels, incoming, taps, ready):
    @pl.when(control[2] == 1)
    def _():
        pltpu.make_async_copy(own_tiles, incoming, ready.at[0]).start()

    @pl.when(control[2] != 1)
    def _():
        pltpu.make_async_copy(arrived, incoming, ready.at[0]).start()

    taps_copy = pltpu.make_async_copy(kernels, taps, ready.at[1])
    taps_copy.start()
    return pltpu.make_async_copy(own_tiles, incoming, ready.at[0]), taps_copy


def forward_kernel(
    control, own_tiles, arrived, kernels, own_in, other_in, own_out, other_out, *rest
):
    rest = rest[-(1 + FORWARD_KEPT * 2 + 9):]
    result, rest = rest[0], rest[1:]
    kept_out, rest = rest[:FORWARD_KEPT], rest[FORWARD_KEPT:]
    kept, rest = rest[:FORWARD_KEPT], rest[FORWARD_KEPT:]
    first_buffer, second_buffer, weight_ready, kept_done, wide, mixed = rest[:6]
    incoming, taps, ready = rest[6:]
    inputs, lows, inverses, slopes, actives = kept
    expand = own_in.shape[1]
    tiles_copy, taps_copy = begin(control, own_tiles, arrived, kernels, incoming, taps, ready)
    loads = []
    for block in range(BLOCKS):
        loads.append(
            (
                fetch(control, block, own_in, other_in, first_buffer, weight_ready.at[block, 0]),
                fetch(control, block, own_out, other_out, second_buffer, weight_ready.at[block, 1]),
            )
        )
    stores = []
    tiles_copy.wait()
    wide[...] = incoming[...].astype(jnp.float32)
    taps_copy.wait()
    for block in range(BLOCKS):
        inputs[block] = wide[...].astype(jnp.bfloat16)
        depthwise_into(wide, taps.at[block], mixed, False)
        values = mixed[...]
        centred = values - jnp.mean(values, axis=-1, keepdims=True)
        inverse = lax.rsqrt(jnp.mean(centred * centred, axis=-1, keepdims=True) + EPSILON)
        inverses[block] = jnp.broadcast_to(inverse, inverses.shape[1:])
        low = (centred * inverse).astype(jnp.bfloat16)
        lows[block] = low
        loads[block][0].wait()
        total = jnp.zeros(wide.shape, jnp.float32)
        for start in range(0, expand, CHUNK):
            part = slice(start, start + CHUNK)
            hidden = jnp.dot(low, first_buffer[block, :, part], preferred_element_type=jnp.float32)
            half = 0.5 * (1.0 + lax.erf(hidden * SQRT_HALF))
            active = (hidden * half).astype(jnp.bfloat16)
            slope = half + hidden * jnp.exp(-0.5 * hidden * hidden) * INV_ROOT_TWO_PI
            slopes[block, :, part] = slope.astype(jnp.bfloat16)
            actives[block, :, part] = active
            if start == 0:
                loads[block][1].wait()
            total = total + jnp.dot(
                active, second_buffer[block, part, :], preferred_element_type=jnp.float32
            )
        wide[...] = (wide[...] + total).astype(jnp.bfloat16).astype(jnp.float32)
        for index in range(FORWARD_KEPT):
            copy = pltpu.make_async_copy(
                kept[index].at[block], kept_out[index].at[block, control[0]], kept_done.at[block, index]
            )
            copy.start()
            stores.append(copy)
    result[...] = wide[...].astype(jnp.bfloat16)
    for copy in stores:
        copy.wait()


def backward_kernel(
    control, seeds, arrived, kernels, lows_all, inverses_all, slopes_all,
    own_in, other_in, own_out, other_out, *rest
):
    rest = rest[-(1 + BACKWARD_KEPT * 2 + 13):]
    result, rest = rest[0], rest[1:]
    kept_out, rest = rest[:BACKWARD_KEPT], rest[BACKWARD_KEPT:]
    kept, rest = rest[:BACKWARD_KEPT], rest[BACKWARD_KEPT:]
    lows, inverses, slopes, known_ready = rest[:4]
    first_buffer, second_buffer, weight_ready, kept_done, wide, spread = rest[4:10]
    incoming, taps, ready = rest[10:]
    ups, hiddens, mixeds = kept
    expand = own_in.shape[1]
    tiles_copy, taps_copy = begin(control, seeds, arrived, kernels, incoming, taps, ready)
    loads = [None] * BLOCKS
    for block in range(BLOCKS - 1, -1, -1):
        second = fetch(control, block, own_out, other_out, second_buffer, weight_ready.at[block, 1])
        known = []
        for index, (source, target) in enumerate(
            ((slopes_all, slopes), (lows_all, lows), (inverses_all, inverses))
        ):
            copy = pltpu.make_async_copy(
                source.at[block, control[0]], target.at[block], known_ready.at[block, index]
            )
            copy.start()
            known.append(copy)
        first = fetch(control, block, own_in, other_in, first_buffer, weight_ready.at[block, 0])
        loads[block] = (second, known, first)
    stores = []
    across = (((1,), (1,)), ((), ()))
    cells = wide.shape[0]
    tiles_copy.wait()
    wide[...] = incoming[:cells, :].astype(jnp.float32)
    taps_copy.wait()
    for block in range(BLOCKS - 1, -1, -1):
        second, known, first = loads[block]
        low = wide[...].astype(jnp.bfloat16)
        ups[block] = low
        total = jnp.zeros(wide.shape, jnp.float32)
        second.wait()
        for copy in known:
            copy.wait()
        for start in range(0, expand, CHUNK):
            part = slice(start, start + CHUNK)
            through = lax.dot_general(
                low, second_buffer[block, part, :], across, preferred_element_type=jnp.float32
            )
            grads = (through * slopes[block, :, part].astype(jnp.float32)).astype(jnp.bfloat16)
            hiddens[block, :, part] = grads
            if start == 0:
                first.wait()
            total = total + lax.dot_general(
                grads, first_buffer[block, :, part], across, preferred_element_type=jnp.float32
            )
        normed = lows[block].astype(jnp.float32)
        mixeds[block] = inverses[block][:, :1] * (
            total
            - jnp.mean(total, axis=-1, keepdims=True)
            - normed * jnp.mean(total * normed, axis=-1, keepdims=True)
        )
        depthwise_into(mixeds.at[block], taps.at[block], spread, True)
        wide[...] = (wide[...] + spread[...]).astype(jnp.bfloat16).astype(jnp.float32)
        for index in range(BACKWARD_KEPT):
            copy = pltpu.make_async_copy(
                kept[index].at[block], kept_out[index].at[block, control[0]], kept_done.at[block, index]
            )
            copy.start()
            stores.append(copy)
    result[:cells, :] = wide[...].astype(jnp.bfloat16)
    result[cells:, :] = incoming[cells:, :]
    for copy in stores:
        copy.wait()


def taps_kernel(inputs, mixed, result):
    steps, cells = inputs.shape[1:3]
    tile = SIDE * SIDE
    for across in range(TAPS):
        sums = [None] * TAPS
        for step in range(steps):
            for start in range(0, cells, tile):
                strips = [pl.ds(start + y * SIDE, SIDE) for y in range(SIDE)]
                rows = [inputs[0, step, strip, :].astype(jnp.float32) for strip in strips]
                moved = [shifted(mixed[0, step, strip, :], REACH - across) for strip in strips]
                for vertical in range(TAPS):
                    for y in range(SIDE):
                        origin = y - (vertical - REACH)
                        if 0 <= origin < SIDE:
                            term = rows[y] * moved[origin]
                            known = sums[vertical]
                            sums[vertical] = term if known is None else known + term
        for vertical in range(TAPS):
            result[0, pl.ds(vertical * TAPS + across, 1), :] = jnp.sum(
                sums[vertical], axis=0, keepdims=True
            )


def call_stage(kernel, name, control, fixed, known, weights, saved, saved_shapes, out_shape):
    scalar = pl.BlockSpec(memory_space=pltpu.SMEM)
    near = pl.BlockSpec(memory_space=pltpu.VMEM)
    far = pl.BlockSpec(memory_space=pl.ANY)
    at_home = lambda value: pltpu.with_memory_space_constraint(value, pltpu.HBM)
    operands = [control, *fixed[:2], *[at_home(value) for value in (*fixed[2:], *known)]]
    operands += [pltpu.with_memory_space_constraint(value, pltpu.VMEM) for value in weights]
    in_specs = [scalar] + [far] * (len(fixed) + len(known) + len(weights))
    aliases = {}
    if saved is not None:
        for index, value in enumerate(saved):
            aliases[len(operands)] = 1 + index
            operands.append(at_home(value))
            in_specs.append(far)

    def buffer(value):
        return pltpu.VMEM((BLOCKS,) + value.shape[2:], value.dtype)

    scratch = [buffer(value) for value in saved_shapes]
    if known:
        lows, inverses, slopes = known
        scratch += [buffer(lows), buffer(inverses), buffer(slopes)]
        scratch += [pltpu.SemaphoreType.DMA((BLOCKS, len(known)))]
    scratch += [
        pltpu.VMEM((BLOCKS,) + weights[0].shape, weights[0].dtype),
        pltpu.VMEM((BLOCKS,) + weights[2].shape, weights[2].dtype),
        pltpu.SemaphoreType.DMA((BLOCKS, 2)),
        pltpu.SemaphoreType.DMA((BLOCKS, len(saved_shapes))),
        pltpu.VMEM((saved_shapes[0].shape[2], out_shape.shape[1]), jnp.float32),
        pltpu.VMEM((saved_shapes[0].shape[2], out_shape.shape[1]), jnp.float32),
        pltpu.VMEM(fixed[0].shape, fixed[0].dtype),
        pltpu.VMEM(fixed[2].shape, fixed[2].dtype),
        pltpu.SemaphoreType.DMA((2,)),
    ]
    outputs = pl.pallas_call(
        kernel,
        name=name,
        out_shape=[out_shape, *[pltpu.HBM(value.shape, value.dtype) for value in saved_shapes]],
        in_specs=in_specs,
        out_specs=[near] + [far] * len(saved_shapes),
        scratch_shapes=scratch,
        input_output_aliases=aliases,
        compiler_params=pltpu.CompilerParams(vmem_limit_bytes=VMEM_LIMIT),
    )(*operands)
    return outputs[0], tuple(outputs[1:])


def tap_grads(inputs, mixed):
    blocks, crops, cells, width = inputs.shape
    window = pl.BlockSpec((1, crops - 1, cells, LANES), lambda block, lane: (block, 0, 0, lane))
    return pl.pallas_call(
        taps_kernel,
        name="taps",
        out_shape=jax.ShapeDtypeStruct((blocks, TAPS * TAPS, width), jnp.float32),
        grid=(blocks, width // LANES),
        in_specs=[window, window],
        out_specs=pl.BlockSpec((1, TAPS * TAPS, LANES), lambda block, lane: (block, 0, lane)),
        compiler_params=pltpu.CompilerParams(vmem_limit_bytes=SMALL_LIMIT),
    )(inputs, mixed)


def head_kernel(*refs):
    finals, (truth, live, weight, seeds) = refs[:-4], refs[-4:]
    step_cells = finals[0].shape[0]
    factor = SIDE * SIDE / (BLOCKS * len(finals) * step_cells)
    head_term = jnp.zeros(weight.shape, jnp.float32)
    loss_term = jnp.zeros((1, 1), jnp.float32)
    for crop, final in enumerate(finals):
        cells = pl.ds(crop * step_cells, step_cells)
        widened = final[...].astype(jnp.float32)
        logits = jnp.sum(widened * weight[...], axis=-1, keepdims=True)
        softplus = jnp.maximum(logits, 0.0) + jnp.log1p(jnp.exp(-jnp.abs(logits)))
        loss = live[cells, :] * (softplus - truth[cells, :] * logits)
        loss_term = loss_term + jnp.sum(loss, axis=0, keepdims=True) * factor
        grads = (jax.nn.sigmoid(logits) - truth[cells, :]) * live[cells, :] * factor
        seeds[crop, :step_cells, :] = (grads * weight[...]).astype(jnp.bfloat16)
        head_term = head_term + jnp.sum(grads * widened, axis=0, keepdims=True)
    place = lax.broadcasted_iota(jnp.int32, (RIDERS, weight.shape[1]), 0)
    riders = jnp.where(place < 2, head_term, jnp.where(place < 4, loss_term, 0.0))
    coarse = riders.astype(jnp.bfloat16)
    rest = (riders - coarse.astype(jnp.float32)).astype(jnp.bfloat16)
    riders = jnp.where(place % 2 == 0, coarse, rest)
    for crop in range(len(finals)):
        seeds[crop, step_cells:, :] = riders


def assemble(control, pieces, distances):
    def kernel(control, *refs):
        sources, result, ready = refs[:-2], refs[-2], refs[-1]
        copies = []
        for source, shards in zip(sources, distances):
            for index, (z_steps, x_steps) in enumerate(shards):
                target = (control[0] - z_steps) % Z_SIZE * X_SIZE + (control[1] - x_steps) % X_SIZE
                copy = pltpu.make_async_copy(
                    source.at[index], result.at[target], ready.at[len(copies)]
                )
                copy.start()
                copies.append(copy)
        for copy in copies:
            copy.wait()

    piece = pieces[0]
    far = pl.BlockSpec(memory_space=pl.ANY)
    return pl.pallas_call(
        kernel,
        name="assemble",
        out_shape=jax.ShapeDtypeStruct((Z_SIZE * X_SIZE,) + piece.shape[1:], piece.dtype),
        in_specs=[pl.BlockSpec(memory_space=pltpu.SMEM)] + [far] * len(pieces),
        out_specs=far,
        scratch_shapes=[pltpu.SemaphoreType.DMA((Z_SIZE * X_SIZE,))],
        compiler_params=pltpu.CompilerParams(vmem_limit_bytes=SMALL_LIMIT),
    )(control, *[pltpu.with_memory_space_constraint(piece, pltpu.HBM) for piece in pieces])


def along_x(value, steps):
    pairs = [
        (z * X_SIZE + x, z * X_SIZE + (x + steps) % X_SIZE)
        for z in range(Z_SIZE)
        for x in range(X_SIZE)
    ]
    return lax.ppermute(value, "dp", pairs)


def along_z(value, steps):
    pairs = [
        (z * X_SIZE + x, (z + steps) % Z_SIZE * X_SIZE + x)
        for z in range(Z_SIZE)
        for x in range(X_SIZE)
    ]
    return lax.ppermute(value, "dp", pairs)


def spread_x(value):
    return [value] + [along_x(value, steps) for steps in range(1, X_SIZE)]


def spread_z(value):
    return [value] + [along_z(value, steps) for steps in range(1, Z_SIZE)]


def chain_x(value):
    half = value.shape[0] // 2
    behind, ahead = along_x(value, 1), along_x(value, -1)
    return [value, behind, along_x(behind[:half], 1), along_x(ahead[half:], -1), ahead]


def chain_z(value):
    half = Z_SIZE // 2
    behind, ahead = [value], [value]
    for step in range(half):
        behind.append(along_z(behind[-1], 1))
        if step < half - 1:
            ahead.append(along_z(ahead[-1], -1))
    return behind + ahead[:0:-1]


def picker(blocks, axis, home):
    count = blocks.shape[axis]
    return lambda steps: lax.dynamic_index_in_dim(
        blocks, (home + steps) % count, axis, keepdims=False
    )


def add(*terms):
    total = terms[0].astype(jnp.float32)
    for term in terms[1:]:
        total = total + term.astype(jnp.float32)
    return total


def collect(blocks, home, along):
    block = picker(blocks, 0, home)
    return add(block(0), *[along(block(steps), steps) for steps in range(1, blocks.shape[0])])


def reduce_x(blocks, axis, home):
    block = picker(blocks, axis, home)
    far, behind, ahead = block(2), block(1), block(-1)
    half = far.shape[0] // 2
    from_behind, from_ahead = along_x(far[:half], 1), along_x(far[half:], -1)
    behind = jnp.concatenate([add(behind[:half], from_behind).astype(jnp.bfloat16), behind[half:]])
    ahead = jnp.concatenate([ahead[:half], add(ahead[half:], from_ahead).astype(jnp.bfloat16)])
    return add(block(0), along_x(behind, 1), along_x(ahead, -1))


def reduce_z(blocks, axis, home):
    block = picker(blocks, axis, home)
    half = Z_SIZE // 2
    behind, ahead = block(half), block(1 - half)
    for steps in range(half - 1, 0, -1):
        behind = add(along_z(behind, 1), block(steps)).astype(jnp.bfloat16)
        if steps < half - 1:
            ahead = add(along_z(ahead, -1), block(-steps)).astype(jnp.bfloat16)
    return add(block(0), along_z(behind, 1), along_z(ahead, -1))


def all_sum(value, axis):
    count = lax.axis_size(axis)
    step = 1
    while step < count:
        value = value + lax.ppermute(value, axis, [(place, place ^ step) for place in range(count)])
        step *= 2
    return value


def outer_sum(left, right):
    return lax.dot_general(
        left, right, (((0, 1), (0, 1)), ((), ())), preferred_element_type=jnp.float32
    )


def body(crop_maps, target_maps, crop_counts, depth_kernels, weight_in, weight_out, head_weight):
    section = lax.axis_index("section")
    sections = lax.axis_size("section")
    stages = sections // BLOCKS
    stage = section // BLOCKS
    core = section % BLOCKS
    micros, slots = crop_maps.shape[1:3]
    width = crop_maps.shape[-1]
    cells = SIDE * SIDE
    other = [(index, index ^ 1) for index in range(sections)]
    onward = [(index, index + BLOCKS) for index in range(sections - BLOCKS)]
    back = [(index + BLOCKS, index) for index in range(sections - BLOCKS)]

    group = lax.axis_index("dp")
    home_z, home_x = group // X_SIZE, group % X_SIZE
    home = jnp.stack([home_z, home_x]).astype(jnp.int32)
    shard_rows, expand = weight_in.shape[1:]
    first_shard = weight_in[0].reshape(shard_rows // 2, 2, expand)
    far_z, far_x = range(Z_SIZE), range(X_SIZE)
    second_column = jnp.stack(spread_z(weight_out[0]))
    first_pieces = chain_z(jnp.stack(spread_x(first_shard)))
    first_places = [[(z, x) for x in far_x] for z in far_z]
    second_pieces = chain_x(second_column)
    ordered = [[(z, x) for z in far_z] for x in far_x]
    second_places = ordered[:2] + [ordered[2][: Z_SIZE // 2], ordered[2][Z_SIZE // 2 :]] + ordered[3:]
    own_out = assemble(home, second_pieces, second_places).reshape(expand, width)
    own_in = assemble(home, first_pieces, first_places).reshape(width, expand)
    other_in = lax.ppermute(own_in, "section", other)
    other_out = lax.ppermute(own_out, "section", other)
    weights = (own_in, other_in, own_out, other_out)
    other_kernel = lax.ppermute(depth_kernels[0], "section", other)
    first_kernel = jnp.where(core == 0, depth_kernels[0], other_kernel)
    second_kernel = jnp.where(core == 0, other_kernel, depth_kernels[0])
    kernels = jnp.stack([first_kernel, second_kernel])

    crops = micros * slots // BLOCKS
    steps = crops // STEP_CROPS
    step_cells = STEP_CROPS * cells
    live = (jnp.arange(slots)[None, :] < crop_counts[0][:, None]).reshape(crops, BLOCKS)
    pick = lambda value: lax.dynamic_index_in_dim(value, core, 1, keepdims=False)
    own_live = pick(live).astype(jnp.float32)[:, None]
    own_crops = pick(crop_maps[0].reshape(crops, BLOCKS, cells, width))
    own_targets = pick(target_maps[0].reshape(crops, BLOCKS, cells))
    entering = own_crops * own_live[:, :, None].astype(jnp.bfloat16)
    entering = entering.reshape(steps, step_cells, width)

    ticks = steps + stages - 1
    spare = steps

    def kept(*tail, dtype):
        return jax.ShapeDtypeStruct((BLOCKS, steps + 1, step_cells) + tail, dtype)

    tile_shape = jax.ShapeDtypeStruct((step_cells, width), jnp.bfloat16)
    forward_shapes = [
        kept(width, dtype=jnp.bfloat16),
        kept(width, dtype=jnp.bfloat16),
        kept(LANES, dtype=jnp.float32),
        kept(expand, dtype=jnp.bfloat16),
        kept(expand, dtype=jnp.bfloat16),
    ]
    saved = None
    arrived = entering[0]
    finals = []
    for moment in range(ticks):
        micro = moment - stage
        place = jnp.where((micro >= 0) & (micro < steps), micro, spare)
        control = jnp.stack([place, core, stage == 0]).astype(jnp.int32)
        result, saved = call_stage(
            forward_kernel, "forward", control,
            [entering[min(moment, steps - 1)], arrived, kernels], [], weights,
            saved, forward_shapes, tile_shape,
        )
        if moment >= stages - 1:
            finals.append(result)
        if moment < ticks - 1:
            arrived = lax.ppermute(result, "section", onward)
    inputs, lows, inverse, slope, active = saved

    is_last = stage == stages - 1
    by_cell = lambda value: value.reshape(crops * cells, 1).astype(jnp.float32)
    seeds = pl.pallas_call(
        head_kernel,
        name="head",
        out_shape=jax.ShapeDtypeStruct((steps, step_cells + RIDERS, width), jnp.bfloat16),
        compiler_params=pltpu.CompilerParams(vmem_limit_bytes=SMALL_LIMIT),
    )(
        *finals,
        by_cell(own_targets),
        by_cell(jnp.broadcast_to(own_live, own_targets.shape)),
        head_weight[None],
    )

    backward_shapes = [
        kept(width, dtype=jnp.bfloat16),
        kept(expand, dtype=jnp.bfloat16),
        kept(width, dtype=jnp.float32),
    ]
    upstream_shape = jax.ShapeDtypeStruct((step_cells + RIDERS, width), jnp.bfloat16)
    grads = None
    arrived = seeds[0]
    for moment in range(ticks):
        micro = moment - (stages - 1 - stage)
        place = jnp.where((micro >= 0) & (micro < steps), micro, spare)
        control = jnp.stack([place, core, is_last]).astype(jnp.int32)
        result, grads = call_stage(
            backward_kernel, "backward", control,
            [seeds[min(moment, steps - 1)], arrived, kernels],
            [lows, inverse, slope], weights, grads, backward_shapes, upstream_shape,
        )
        if moment < ticks - 1:
            arrived = lax.ppermute(result, "section", back)
    ups, hidden_grads, mixed_grads = grads

    taps = tap_grads(inputs, mixed_grads)
    riders = result[step_cells : step_cells + 4].astype(jnp.float32)
    riders = jnp.stack([riders[0] + riders[1], riders[2] + riders[3]])
    tap_of = lambda which: jnp.concatenate(
        [lax.dynamic_index_in_dim(taps, which, 0, keepdims=False), riders]
    )
    small_home, small_away, hidden_grads, ups = lax.optimization_barrier(
        (tap_of(core), tap_of(1 - core), hidden_grads, ups)
    )
    small = small_home + lax.ppermute(small_away, "section", other)

    def block_of(value, which):
        return lax.dynamic_index_in_dim(value, which, 0, keepdims=False)[:steps]

    def outer_in(which):
        return outer_sum(block_of(lows, which), block_of(hidden_grads, which))

    def outer_out(which):
        return outer_sum(block_of(active, which), block_of(ups, which))

    came_out = lax.ppermute(outer_out(1 - core).astype(jnp.bfloat16), "section", other)
    came_in = lax.ppermute(outer_in(1 - core).astype(jnp.bfloat16), "section", other)
    by_group = lambda value, *tail: value.astype(jnp.bfloat16).reshape((Z_SIZE, X_SIZE) + tail)
    sum_out = outer_out(core) + came_out.astype(jnp.float32)
    sum_out = by_group(sum_out, expand // Z_SIZE // X_SIZE, width)
    sum_in = by_group(outer_in(core) + came_in.astype(jnp.float32), *first_shard.shape)
    small, sum_in, sum_out = lax.optimization_barrier((small, sum_in, sum_out))

    second_part = reduce_z(sum_out, 0, home_z).astype(jnp.bfloat16)
    first_part = reduce_x(sum_in, 1, home_x).astype(jnp.bfloat16)
    second_part = collect(second_part, home_x, along_x)
    first_part = collect(first_part, home_z, along_z).reshape(shard_rows, expand)
    small = all_sum(small, "dp")
    tap_count = TAPS * TAPS
    return (
        first_part[None],
        second_part[None],
        small[None, :tap_count],
        small[tap_count],
        small[tap_count + 1, 0],
    )


def solution(mesh):
    return jax.shard_map(
        body,
        mesh=mesh,
        in_specs=(
            P("dp", None, None, None, None, None),
            P("dp", None, None, None, None),
            P("dp", None),
            P("section", None, None),
            P("section", "dp", None),
            P("section", "dp", None),
            P(),
        ),
        out_specs=(
            P("section", "dp", None),
            P("section", "dp", None),
            P("section", None, None),
            P(),
            P(),
        ),
        check_vma=False,
    )
```
